32 devices in a mesh: dp: 2 (over x), expert: 16 (over z, y, core).
Axes of the slice: x: 2, y: 2, z: 4, core: 2. Of those that a mesh axis runs over, the one named last changes fastest.
Arguments:
- tokens: bfloat16 [2, 256, 2048], P('dp', 'expert'), may hold values from -6 to 6
- cotangent: bfloat16 [2, 256, 2048], P('dp', 'expert'), may hold values from -1.5 to 1.5
- routes: int32 [2, 256], P(None, 'expert'), may hold values from 0 to 15, as said below
- gate_prob: bfloat16 [2, 256], P(None, 'expert'), may hold values from 0.19921875 to 1
- w_gate: bfloat16 [16, 768, 2048], P('expert', 'dp'), may hold values from -0.125 to 0.125
- w_up: bfloat16 [16, 768, 2048], P('expert', 'dp'), may hold values from -0.125 to 0.125
- w_down: bfloat16 [16, 768, 2048], P('expert', 'dp'), may hold values from -0.21875 to 0.21875
Outputs:
- grad_tokens: bfloat16 [2, 256, 2048], P('dp', 'expert')
- grad_prob: float32 [2, 256], P('dp', 'expert')
- grad_w_gate: bfloat16 [16, 768, 2048], P('expert', 'dp')
- grad_w_up: bfloat16 [16, 768, 2048], P('expert', 'dp')
- grad_w_down: bfloat16 [16, 768, 2048], P('expert', 'dp')
The draws below stay inside these ranges and needn't reach their ends.
Inputs may be any that keep to these rules, and one draw needn't show every extreme that they name: `routes`: one expert, the same for the whole micro-batch, is named by exactly 4 of the 16 tokens of every device (tokens[d, e * 16 : (e + 1) * 16] for each d and e). Of the 32 tokens with one index e of the expert axis, at most 3 name any other single expert, and one other expert, the same for every e, is named by exactly 3 of them.
All inputs are finite; a program needn't handle non-finite values.
Results may differ from the reference program's by a relative error of at most 0.0065.
Values may be sent and summed in bfloat16 or wider, within the bound.
No kernel may reach another device: no remote copies, remote signals or barrier semaphores. Data moves between devices by JAX's collectives and lax.ppermute only.
A program may use at most 64 MiB of HBM per device.

```python
import jax
import jax.numpy as jnp
from jax import lax

D = 2048
H = 768
TOK_DEV = 16
EXPERTS = 16
ROW_TOK = 256
HOT_TOK = 4
REG_DEV = 12
CAP = 3
N_DP = 2
N_EXPERT = 16


def routing_table(key):
    hot_id = jax.random.randint(jax.random.fold_in(key, 11), (), 0, EXPERTS).astype(jnp.int32)
    full_id = jax.random.randint(jax.random.fold_in(key, 12), (), 0, EXPERTS - 1).astype(jnp.int32)
    group_regular = N_DP * REG_DEV
    others = jnp.arange(EXPERTS - 2, dtype=jnp.int32)
    others = others + (others >= full_id).astype(jnp.int32)
    pool = jnp.repeat(others, CAP)
    head = jnp.full((CAP,), full_id, jnp.int32)

    def one_group(group_key):
        mixed = jax.random.permutation(jax.random.fold_in(group_key, 1), pool)
        chosen = jnp.concatenate([head, mixed[:group_regular - CAP]])
        chosen = jax.random.permutation(jax.random.fold_in(group_key, 2), chosen)
        named = (hot_id + 1 + chosen) % EXPERTS
        device_keys = jax.random.split(jax.random.fold_in(group_key, 3), N_DP)

        def one_device(device_key, device):
            place = jax.random.permutation(device_key, TOK_DEV).astype(jnp.int32)
            is_hot = place < HOT_TOK
            pick = jnp.clip(place - HOT_TOK, 0, REG_DEV - 1) + device * REG_DEV
            return jnp.where(is_hot, hot_id, named[pick]).astype(jnp.int32)
        return jax.vmap(one_device)(device_keys, jnp.arange(N_DP, dtype=jnp.int32))
    group_keys = jax.random.split(jax.random.fold_in(key, 13), EXPERTS)
    table = jax.vmap(one_group)(group_keys)
    table = jnp.transpose(table, (1, 0, 2)).reshape(N_DP, EXPERTS * TOK_DEV)
    return table.astype(jnp.int32)


def draw_routes(key, part):
    return routing_table(key)


def levels(stream_key, extent, cuts, smallest, high):
    def one(dim, blocks):
        steps = jax.random.uniform(jax.random.fold_in(jax.random.fold_in(stream_key, 6), dim), (blocks,), jnp.float32, smallest / len(cuts), high / len(cuts))
        return jnp.repeat(jnp.exp(steps), extent[dim] // blocks).reshape((-1,) + (1,) * (len(extent) - dim - 1))

    gain = one(*cuts[0])
    for cut in cuts[1:]:
        gain = gain * one(*cut)
    return gain


def normal_values(rng, dims, deviation, bound, pieces=(), kind=jnp.bfloat16):
    entries = deviation * jax.random.normal(rng, dims, jnp.float32)
    if pieces:
        entries = entries * levels(rng, dims, pieces, -0.22, 0.18)
    return jnp.clip(entries, -bound, bound).astype(kind)


def setup_inputs(seed: int = 0) -> dict:
    key_list = jax.random.split(jax.random.key(seed), 8)
    return {
        "tokens": normal_values(key_list[0], (N_DP, ROW_TOK, D), 1.0, 6.0, ((0, 2), (1, 16))),
        "cotangent": normal_values(key_list[1], (N_DP, ROW_TOK, D), 0.25, 1.5, ((0, 2), (1, 16))),
        "routes": draw_routes(jax.random.fold_in(key_list[7], 71), 0),
        "gate_prob": jnp.clip(0.19921875 + 0.80078125 * jax.random.uniform(key_list[3], (N_DP, ROW_TOK), jnp.float32) ** levels(key_list[3], (N_DP, ROW_TOK), ((1, 16),), -0.2, 0.2), 0.19921875, 1.0).astype(jnp.bfloat16),
        "w_gate": normal_values(key_list[4], (EXPERTS, H, D), D ** -0.5, 0.125, ((0, 16), (1, 2))),
        "w_up": normal_values(key_list[5], (EXPERTS, H, D), D ** -0.5, 0.125, ((0, 16), (1, 2))),
        "w_down": normal_values(key_list[6], (EXPERTS, H, D), H ** -0.5, 0.21875, ((0, 16), (1, 2))),
    }


def silu_parts(gate_pre):
    sigma = jax.nn.sigmoid(gate_pre)
    return gate_pre * sigma, sigma * (1.0 + gate_pre * (1.0 - sigma))


def expert_backward(rows_x, rows_dy, rows_p, gate_w, up_w, down_w):
    row_count = rows_x.shape[0]
    hid_dev = gate_w.shape[0] // N_DP
    gate_pre = jnp.dot(rows_x, gate_w.T, preferred_element_type=jnp.float32)
    up_pre = jnp.dot(rows_x, up_w.T, preferred_element_type=jnp.float32)
    swish_val, swish_slope = silu_parts(gate_pre)
    active = swish_val * up_pre
    weight = rows_p.astype(jnp.float32)[:, None]
    scaled_act = (weight * active).astype(jnp.bfloat16)
    back_proj = jnp.dot(rows_dy, down_w.T, preferred_element_type=jnp.float32)
    d_active = weight * back_proj
    d_gate = (d_active * up_pre * swish_slope).astype(jnp.bfloat16)
    d_up = (d_active * swish_val).astype(jnp.bfloat16)
    block_terms = jnp.sum((active * back_proj).reshape(row_count, N_DP, hid_dev), axis=2)
    block_terms = lax.optimization_barrier(block_terms.astype(jnp.bfloat16))
    prob_grad = jnp.sum(block_terms.astype(jnp.float32), axis=1)
    feature_grad = jnp.zeros((row_count, rows_x.shape[1]), jnp.float32)
    for hid_block in range(N_DP):
        low_edge = hid_block * hid_dev
        high_edge = low_edge + hid_dev
        block_part = jnp.dot(d_gate[:, low_edge:high_edge], gate_w[low_edge:high_edge], preferred_element_type=jnp.float32)
        block_part = block_part + jnp.dot(d_up[:, low_edge:high_edge], up_w[low_edge:high_edge], preferred_element_type=jnp.float32)
        block_part = lax.optimization_barrier(block_part.astype(jnp.bfloat16))
        feature_grad = feature_grad + block_part.astype(jnp.float32)
    weight_grads = (
        jnp.dot(d_gate.T, rows_x, preferred_element_type=jnp.float32),
        jnp.dot(d_up.T, rows_x, preferred_element_type=jnp.float32),
        jnp.dot(scaled_act.T, rows_dy, preferred_element_type=jnp.float32),
    )
    return weight_grads, feature_grad, prob_grad


def reference(tokens, cotangent, routes, gate_prob, w_gate, w_up, w_down):
    features = tokens.shape[2]
    flat_x = tokens.reshape(-1, features)
    flat_dy = cotangent.reshape(-1, features)
    flat_route = routes.reshape(-1).astype(jnp.int32)
    flat_prob = gate_prob.reshape(-1)
    token_count = flat_route.shape[0]
    expert_ids = jnp.arange(EXPERTS, dtype=jnp.int32)
    counts = jnp.sum((flat_route[:, None] == expert_ids[None, :]).astype(jnp.int32), axis=0).astype(jnp.int32)
    hot_id = jnp.argmax(counts).astype(jnp.int32)
    starts = (jnp.cumsum(counts) - counts).astype(jnp.int32)
    sort_order = jnp.argsort(flat_route, stable=True).astype(jnp.int32)
    reg_span = N_EXPERT * CAP
    hot_span = N_DP * N_EXPERT * HOT_TOK
    pad_rows = reg_span + hot_span
    sorted_x = jnp.concatenate([flat_x[sort_order], jnp.zeros((pad_rows, features), flat_x.dtype)], axis=0)
    sorted_dy = jnp.concatenate([flat_dy[sort_order], jnp.zeros((pad_rows, features), flat_dy.dtype)], axis=0)
    sorted_prob = jnp.concatenate([flat_prob[sort_order], jnp.zeros((pad_rows,), flat_prob.dtype)], axis=0)

    def regular(packed):
        expert, gate_w, up_w, down_w = packed
        first_row = starts[expert]
        is_live = (jnp.arange(reg_span, dtype=jnp.int32) < counts[expert]) & (expert != hot_id)
        rows_x = lax.dynamic_slice_in_dim(sorted_x, first_row, reg_span, 0)
        rows_dy = lax.dynamic_slice_in_dim(sorted_dy, first_row, reg_span, 0)
        rows_p = lax.dynamic_slice_in_dim(sorted_prob, first_row, reg_span, 0)
        rows_p = jnp.where(is_live, rows_p, jnp.zeros_like(rows_p))
        return expert_backward(rows_x, rows_dy, rows_p, gate_w, up_w, down_w)

    reg_grads, reg_feature, reg_prob = lax.map(regular, (expert_ids, w_gate, w_up, w_down))
    hot_first = starts[hot_id]
    hot_x = lax.dynamic_slice_in_dim(sorted_x, hot_first, hot_span, 0)
    hot_dy = lax.dynamic_slice_in_dim(sorted_dy, hot_first, hot_span, 0)
    hot_p = lax.dynamic_slice_in_dim(sorted_prob, hot_first, hot_span, 0)
    hot_grads, hot_feature, hot_prob = expert_backward(hot_x, hot_dy, hot_p, w_gate[hot_id], w_up[hot_id], w_down[hot_id])
    sorted_route = flat_route[sort_order]
    position = (jnp.arange(token_count, dtype=jnp.int32) - starts[sorted_route]).astype(jnp.int32)
    is_hot = sorted_route == hot_id
    reg_pos = jnp.clip(position, 0, reg_span - 1)
    hot_pos = jnp.clip(position, 0, hot_span - 1)
    feature_sorted = jnp.where(is_hot[:, None], hot_feature[hot_pos], reg_feature[sorted_route, reg_pos])
    prob_sorted = jnp.where(is_hot, hot_prob[hot_pos], reg_prob[sorted_route, reg_pos])
    grad_tokens = jnp.zeros_like(feature_sorted).at[sort_order].set(feature_sorted)
    grad_prob = jnp.zeros_like(prob_sorted).at[sort_order].set(prob_sorted)
    is_hot_expert = (expert_ids == hot_id)[:, None, None]
    grad_w_gate = jnp.where(is_hot_expert, hot_grads[0][None], reg_grads[0]).astype(jnp.bfloat16)
    grad_w_up = jnp.where(is_hot_expert, hot_grads[1][None], reg_grads[1]).astype(jnp.bfloat16)
    grad_w_down = jnp.where(is_hot_expert, hot_grads[2][None], reg_grads[2]).astype(jnp.bfloat16)
    return (grad_tokens.astype(jnp.bfloat16).reshape(tokens.shape), grad_prob.reshape(gate_prob.shape), grad_w_gate, grad_w_up, grad_w_down)
```

```python
import jax
import jax.numpy as jnp
from jax import lax
from jax.sharding import PartitionSpec as P

AXES = ("dp", "expert")
LANES = 128


def body(tokens, cotangent, routes, gate_prob, w_gate, w_up, w_down):
    groups = lax.axis_size("dp")
    experts = lax.axis_size("expert")
    tok_dev = tokens.shape[1]
    features = tokens.shape[2]
    slots = tok_dev // 4
    rows = groups * experts * slots
    f32, bf16 = jnp.float32, jnp.bfloat16
    mine = lax.axis_index("dp")

    route = lax.dynamic_index_in_dim(routes, mine, 0, keepdims=False)
    prob = lax.dynamic_index_in_dim(gate_prob, mine, 0, keepdims=False)
    token_ids = jnp.arange(tok_dev, dtype=jnp.int32)
    same = route[:, None] == route[None, :]
    earlier = same & (token_ids[None, :] < token_ids[:, None])
    rank = jnp.sum(earlier.astype(jnp.int32), axis=1)
    slot = route * slots + rank
    slot_ids = jnp.arange(experts * slots, dtype=jnp.int32)
    pick = (slot[:, None] == slot_ids[None, :]).astype(bf16)

    packed = jnp.concatenate(
        [tokens[0], cotangent[0], jnp.broadcast_to(prob[:, None], (tok_dev, LANES))], axis=1
    )
    send = jnp.dot(pick.T, packed, preferred_element_type=f32).astype(bf16)
    send = send.reshape(1, experts, slots, packed.shape[1])
    send = jnp.broadcast_to(send, (groups,) + send.shape[1:])
    send = send.reshape(groups * experts, slots, packed.shape[1])
    got = lax.all_to_all(send, AXES, split_axis=0, concat_axis=0, tiled=True)
    got = got.reshape(rows, packed.shape[1])
    rows_x = got[:, :features]
    rows_dy = got[:, features : 2 * features]
    weight = got[:, 2 * features : 2 * features + 1].astype(f32)

    gate_w, up_w, down_w = w_gate[0], w_up[0], w_down[0]
    gate_pre = jnp.einsum("rd,hd->rh", rows_x, gate_w, preferred_element_type=f32)
    up_pre = jnp.einsum("rd,hd->rh", rows_x, up_w, preferred_element_type=f32)
    back_proj = jnp.einsum("rd,hd->rh", rows_dy, down_w, preferred_element_type=f32)
    sigma = jax.nn.sigmoid(gate_pre)
    swish = gate_pre * sigma
    slope = sigma * (1.0 + gate_pre * (1.0 - sigma))
    active = swish * up_pre
    scaled_act = (weight * active).astype(bf16)
    d_active = weight * back_proj
    d_gate = (d_active * up_pre * slope).astype(bf16)
    d_up = (d_active * swish).astype(bf16)
    prob_part = jnp.sum(active * back_proj, axis=1, keepdims=True).astype(bf16)
    feature_part = jnp.dot(d_gate, gate_w, preferred_element_type=f32)
    feature_part = feature_part + jnp.dot(d_up, up_w, preferred_element_type=f32)
    reply = jnp.concatenate(
        [feature_part.astype(bf16), jnp.broadcast_to(prob_part, (rows, LANES))], axis=1
    )
    reply = reply.reshape(groups * experts, slots, features + LANES)
    back = lax.all_to_all(reply, AXES, split_axis=0, concat_axis=0, tiled=True)
    back = back.reshape(rows, features + LANES)
    total = jnp.dot(jnp.tile(pick, (1, groups)), back, preferred_element_type=f32)

    grad_w_gate = jnp.einsum("rh,rd->hd", d_gate, rows_x, preferred_element_type=f32)
    grad_w_up = jnp.einsum("rh,rd->hd", d_up, rows_x, preferred_element_type=f32)
    grad_w_down = jnp.einsum("rh,rd->hd", scaled_act, rows_dy, preferred_element_type=f32)
    return (
        total[None, :, :features].astype(bf16),
        total[None, :, features],
        grad_w_gate.astype(bf16)[None],
        grad_w_up.astype(bf16)[None],
        grad_w_down.astype(bf16)[None],
    )


def solution(mesh):
    in_specs = (
        P("dp", "expert", None),
        P("dp", "expert", None),
        P(None, "expert"),
        P(None, "expert"),
        P("expert", "dp", None),
        P("expert", "dp", None),
        P("expert", "dp", None),
    )
    out_specs = (
        P("dp", "expert", None),
        P("dp", "expert"),
        P("expert", "dp", None),
        P("expert", "dp", None),
        P("expert", "dp", None),
    )
    return jax.shard_map(body, mesh=mesh, in_specs=in_specs, out_specs=out_specs, check_vma=False)
```

```python
import jax
import jax.numpy as jnp
from jax import lax
from jax.experimental import pallas as pl
from jax.experimental.pallas import tpu as pltpu
from jax.sharding import PartitionSpec as P

AXES = ("dp", "expert")
LANES = 128
F32, BF16 = jnp.float32, jnp.bfloat16
VMEM = pl.BlockSpec(memory_space=pltpu.VMEM)
SMEM = pl.BlockSpec(memory_space=pltpu.SMEM)


def dot(a, b, dims):
    return lax.dot_general(a, b, ((dims[:1], dims[1:]), ((), ())), preferred_element_type=F32)


def pack_kernel(slots, mine_ref, route_s, route_v, prob_v, tok_ref, cot_ref, send_ref, pick_ref):
    mine = mine_ref[0]
    tok_dev, features = tok_ref.shape
    block = pick_ref.shape[0]
    groups = send_ref.shape[0] // block
    own = lax.broadcasted_iota(jnp.int32, route_v.shape, 0) == mine
    route = jnp.sum(jnp.where(own, route_v[...], 0), axis=0, keepdims=True)
    prob = jnp.sum(jnp.where(own, prob_v[...].astype(F32), 0.0), axis=0, keepdims=True)
    token = lax.broadcasted_iota(jnp.int32, (1, tok_dev), 1)
    rank = jnp.zeros((1, tok_dev), jnp.int32)
    for t in range(tok_dev):
        rank += ((route == route_s[mine, t]) & (token > t)).astype(jnp.int32)
    target = route * (2 * slots) + rank
    row = lax.broadcasted_iota(jnp.int32, (block, tok_dev), 0)
    pick_x = (row == target).astype(F32)
    pick_y = (row == target + slots).astype(F32)
    weight = jnp.sum(pick_x * prob, axis=1, keepdims=True)
    pick_x, pick_y = pick_x.astype(BF16), pick_y.astype(BF16)
    pick_ref[:, :tok_dev] = pick_x
    pick_ref[:, tok_dev:] = pick_y
    sent = dot(pick_x, tok_ref[...], (1, 0)) + dot(pick_y, cot_ref[...], (1, 0))
    sent = sent.astype(BF16)
    weight = jnp.broadcast_to(weight, (block, LANES)).astype(BF16)
    for g in range(groups):
        send_ref[g * block : (g + 1) * block, :features] = sent
        send_ref[g * block : (g + 1) * block, features:] = weight


def expert_kernel(slots, chunk, got_ref, gate_ref, up_ref, down_ref, reply_ref, dg_ref, du_ref, sa_ref):
    features = gate_ref.shape[1]
    half = features // 2

    @pl.loop(0, got_ref.shape[0] // chunk)
    def _(step):
        at = pl.ds(pl.multiple_of(step * chunk, chunk), chunk)
        data = got_ref[at, :features]
        weight = got_ref[at, features : features + 1].astype(F32)
        gate_pre = dot(data, gate_ref[...], (1, 1))
        up_pre = dot(data, up_ref[...], (1, 1))
        back_proj = dot(data, down_ref[...], (1, 1))
        back_proj = pltpu.roll(back_proj, chunk - slots, 0)
        sigma = jax.nn.sigmoid(gate_pre)
        swish = gate_pre * sigma
        slope = sigma * (1.0 + gate_pre * (1.0 - sigma))
        active = swish * up_pre
        scaled = weight * active
        d_active = weight * back_proj
        d_gate = d_active * up_pre * slope
        d_up = d_active * swish
        part = jnp.sum(active * back_proj, axis=1, keepdims=True)
        dg, dg_low = d_gate.astype(BF16), pltpu.roll(d_gate, slots, 0).astype(BF16)
        du, du_low = d_up.astype(BF16), pltpu.roll(d_up, slots, 0).astype(BF16)
        dg_ref[at, :] = dg
        du_ref[at, :] = du
        sa_ref[at, :] = pltpu.roll(scaled, slots, 0).astype(BF16)
        grad = dot(dg, gate_ref[:, :half], (1, 0)) + dot(du, up_ref[:, :half], (1, 0))
        grad += dot(dg_low, gate_ref[:, half:], (1, 0)) + dot(du_low, up_ref[:, half:], (1, 0))
        reply_ref[at, :half] = grad.astype(BF16)
        reply_ref[at, half:] = jnp.broadcast_to(part, (chunk, LANES)).astype(BF16)


def unpack_kernel(pick_ref, back_ref, tok_ref, prob_ref):
    tok_dev, features = tok_ref.shape
    half = features // 2
    total = dot(pick_ref[...], back_ref[...], (1, 0))
    tok_ref[:, :half] = total[:tok_dev, :half].astype(BF16)
    tok_ref[:, half:] = total[tok_dev:, :half].astype(BF16)
    part = total[:tok_dev, half:]
    here = lax.broadcasted_iota(jnp.int32, part.shape, 0)
    diagonal = here == lax.broadcasted_iota(jnp.int32, part.shape, 1)
    part = jnp.sum(jnp.where(diagonal, part, 0.0), axis=0, keepdims=True)
    prob_ref[...] = part[:, :tok_dev]


def call(kernel, in_specs, outs, *args):
    return pl.pallas_call(
        kernel,
        in_specs=in_specs,
        out_specs=[VMEM] * len(outs),
        out_shape=[jax.ShapeDtypeStruct(s, d) for s, d in outs],
        compiler_params=pltpu.CompilerParams(vmem_limit_bytes=48 << 20),
    )(*args)


def body(tokens, cotangent, routes, gate_prob, w_gate, w_up, w_down):
    groups = lax.axis_size("dp")
    experts = lax.axis_size("expert")
    _, tok_dev, features = tokens.shape
    hidden = w_gate.shape[1]
    half = features // 2
    slots = tok_dev // 4
    block = experts * 2 * slots
    rows = groups * block
    chunk = min(rows, 256)
    mine = lax.axis_index("dp").astype(jnp.int32).reshape(1)

    send, pick = call(
        lambda *refs: pack_kernel(slots, *refs),
        [SMEM, SMEM, VMEM, VMEM, VMEM, VMEM],
        [((rows, features + LANES), BF16), ((block, 2 * tok_dev), BF16)],
        mine, routes, routes, gate_prob, tokens[0], cotangent[0],
    )
    got = lax.all_to_all(send, AXES, split_axis=0, concat_axis=0, tiled=True)
    reply, d_gate, d_up, scaled_act = call(
        lambda *refs: expert_kernel(slots, chunk, *refs),
        [VMEM] * 4,
        [((rows, half + LANES), BF16)] + [((rows, hidden), BF16)] * 3,
        got, w_gate[0], w_up[0], w_down[0],
    )
    back = lax.all_to_all(reply, AXES, split_axis=0, concat_axis=0, tiled=True)
    grad_tokens, grad_prob = call(
        unpack_kernel,
        [VMEM] * 2,
        [((tok_dev, features), BF16), ((1, tok_dev), F32)],
        jnp.tile(pick.T, (1, groups)), back,
    )
    data = got[:, :features]
    weight_grads = [
        jnp.einsum("rh,rd->hd", left, data, preferred_element_type=F32).astype(BF16)[None]
        for left in (d_gate, d_up, scaled_act)
    ]
    return (grad_tokens[None], grad_prob, *weight_grads)


def solution(mesh):
    in_specs = (
        P("dp", "expert", None),
        P("dp", "expert", None),
        P(None, "expert"),
        P(None, "expert"),
        P("expert", "dp", None),
        P("expert", "dp", None),
        P("expert", "dp", None),
    )
    out_specs = (
        P("dp", "expert", None),
        P("dp", "expert"),
        P("expert", "dp", None),
        P("expert", "dp", None),
        P("expert", "dp", None),
    )
    return jax.shard_map(body, mesh=mesh, in_specs=in_specs, out_specs=out_specs, check_vma=False)
```

```python
import jax
import jax.numpy as jnp
from jax import lax
from jax.experimental import pallas as pl
from jax.experimental.pallas import tpu as pltpu
from jax.sharding import PartitionSpec as P

AXES = ("dp", "expert")
LANES = 128
F32, BF16 = jnp.float32, jnp.bfloat16
VMEM = pl.BlockSpec(memory_space=pltpu.VMEM)
HBM = pl.BlockSpec(memory_space=pltpu.HBM)


def dot(a, b, dims):
    return lax.dot_general(a, b, ((dims[:1], dims[1:]), ((), ())), preferred_element_type=F32)


def pack_kernel(slots, *refs):
    ins, (send_ref, pick_ref), kept, bufs, sems = refs[:7], refs[7:9], refs[9:12], refs[12:16], refs[16]
    copies = [
        pltpu.make_async_copy(a, b, sems.at[i]) for i, (a, b) in enumerate(zip(ins, bufs + kept))
    ]
    for copy in copies:
        copy.start()
    route_v, prob_v, tok_ref, cot_ref = bufs
    tok_dev, features = tok_ref.shape
    block = pick_ref.shape[0]
    groups = send_ref.shape[0] // block
    mine = lax.axis_index("dp")
    own = lax.broadcasted_iota(jnp.int32, route_v.shape, 0) == mine
    copies[0].wait()
    route = jnp.sum(jnp.where(own, route_v[...], 0), axis=0, keepdims=True)
    copies[1].wait()
    prob = jnp.sum(jnp.where(own, prob_v[...].astype(F32), 0.0), axis=0, keepdims=True)
    here = lax.broadcasted_iota(jnp.int32, (tok_dev, tok_dev), 0)
    there = lax.broadcasted_iota(jnp.int32, (tok_dev, tok_dev), 1)
    column = jnp.sum(jnp.where(here == there, route, 0), axis=1, keepdims=True)
    rank = jnp.sum(((column == route) & (here < there)).astype(jnp.int32), axis=0, keepdims=True)
    target = route * (2 * slots) + rank
    row = lax.broadcasted_iota(jnp.int32, (block, tok_dev), 0)
    pick_x = (row == target).astype(F32)
    pick_y = (row == target + slots).astype(F32)
    weight = jnp.sum(pick_x * prob, axis=1, keepdims=True)
    pick_x, pick_y = pick_x.astype(BF16), pick_y.astype(BF16)
    pick_ref[:, :tok_dev] = pick_x
    pick_ref[:, tok_dev:] = pick_y
    copies[2].wait()
    copies[3].wait()
    sent = dot(pick_x, tok_ref[...], (1, 0)) + dot(pick_y, cot_ref[...], (1, 0))
    sent = sent.astype(BF16)
    weight = jnp.broadcast_to(weight, (block, LANES)).astype(BF16)
    for g in range(groups):
        send_ref[g * block : (g + 1) * block, :features] = sent
        send_ref[g * block : (g + 1) * block, features:] = weight
    for copy in copies[4:]:
        copy.wait()


def expert_kernel(slots, chunk, got_ref, gate_ref, up_ref, down_ref, reply_ref, dg_ref, du_ref, sa_ref):
    features = gate_ref.shape[1]
    half = features // 2

    @pl.loop(0, got_ref.shape[0] // chunk)
    def _(step):
        at = pl.ds(pl.multiple_of(step * chunk, chunk), chunk)
        data = got_ref[at, :features]
        weight = got_ref[at, features : features + 1].astype(F32)
        gate_pre = dot(data, gate_ref[...], (1, 1))
        up_pre = dot(data, up_ref[...], (1, 1))
        back_proj = dot(data, down_ref[...], (1, 1))
        back_proj = pltpu.roll(back_proj, chunk - slots, 0)
        sigma = jax.nn.sigmoid(gate_pre)
        swish = gate_pre * sigma
        slope = sigma * (1.0 + gate_pre * (1.0 - sigma))
        active = swish * up_pre
        scaled = weight * active
        d_active = weight * back_proj
        d_gate = d_active * up_pre * slope
        d_up = d_active * swish
        part = jnp.sum(active * back_proj, axis=1, keepdims=True)
        dg, dg_low = d_gate.astype(BF16), pltpu.roll(d_gate, slots, 0).astype(BF16)
        du, du_low = d_up.astype(BF16), pltpu.roll(d_up, slots, 0).astype(BF16)
        dg_ref[at, :] = dg
        du_ref[at, :] = du
        sa_ref[at, :] = pltpu.roll(scaled, slots, 0).astype(BF16)
        grad = dot(dg, gate_ref[:, :half], (1, 0)) + dot(du, up_ref[:, :half], (1, 0))
        grad += dot(dg_low, gate_ref[:, half:], (1, 0)) + dot(du_low, up_ref[:, half:], (1, 0))
        reply_ref[at, :half] = grad.astype(BF16)
        reply_ref[at, half:] = jnp.broadcast_to(part, (chunk, LANES)).astype(BF16)


def unpack_kernel(pick_ref, back_ref, tok_ref, prob_ref):
    tok_dev, features = tok_ref.shape
    half = features // 2
    total = dot(pick_ref[...], back_ref[...], (1, 0))
    tok_ref[:, :half] = total[:tok_dev, :half].astype(BF16)
    tok_ref[:, half:] = total[tok_dev:, :half].astype(BF16)
    part = total[:tok_dev, half:]
    here = lax.broadcasted_iota(jnp.int32, part.shape, 0)
    diagonal = here == lax.broadcasted_iota(jnp.int32, part.shape, 1)
    part = jnp.sum(jnp.where(diagonal, part, 0.0), axis=0, keepdims=True)
    prob_ref[...] = part[:, :tok_dev]


def near(shape, dtype=BF16):
    small = shape[0] * shape[1] <= 1 << 20
    return pltpu.VMEM(shape, dtype) if small else jax.ShapeDtypeStruct(shape, dtype)


def fetched(array):
    small = array.size <= 1 << 20
    return pltpu.with_memory_space_constraint(array, pltpu.VMEM) if small else array


def call(kernel, in_specs, outs, *args, scratch=()):
    return pl.pallas_call(
        kernel,
        in_specs=in_specs,
        scratch_shapes=scratch,
        out_specs=[VMEM] * len(outs),
        out_shape=outs,
        compiler_params=pltpu.CompilerParams(vmem_limit_bytes=48 << 20),
    )(*args)


def body(tokens, cotangent, routes, gate_prob, w_gate, w_up, w_down):
    groups = lax.axis_size("dp")
    experts = lax.axis_size("expert")
    _, tok_dev, features = tokens.shape
    hidden = w_gate.shape[1]
    half = features // 2
    slots = tok_dev // 4
    block = experts * 2 * slots
    rows = groups * block
    chunk = min(rows, 256)
    operands = (routes, gate_prob, tokens[0], cotangent[0], w_gate[0], w_up[0], w_down[0])

    send, pick, *weights = call(
        lambda *refs: pack_kernel(slots, *refs),
        [HBM] * 7,
        [near((rows, features + LANES)), near((block, 2 * tok_dev))]
        + [near((hidden, features))] * 3,
        *[pltpu.with_memory_space_constraint(a, pltpu.HBM) for a in operands],
        scratch=[pltpu.VMEM(a.shape, a.dtype) for a in operands[:4]]
        + [pltpu.SemaphoreType.DMA((7,))],
    )
    got = lax.all_to_all(send, AXES, split_axis=0, concat_axis=0, tiled=True)
    reply, d_gate, d_up, scaled_act = call(
        lambda *refs: expert_kernel(slots, chunk, *refs),
        [VMEM] * 4,
        [near((rows, half + LANES))] + [near((rows, hidden))] * 3,
        *[fetched(a) for a in (got, *weights)],
    )
    back = lax.all_to_all(reply, AXES, split_axis=0, concat_axis=0, tiled=True)
    grad_tokens, grad_prob = call(
        unpack_kernel,
        [VMEM] * 2,
        [jax.ShapeDtypeStruct((tok_dev, features), BF16), jax.ShapeDtypeStruct((1, tok_dev), F32)],
        jnp.tile(pick.T, (1, groups)), back,
    )
    data = got[:, :features]
    weight_grads = [
        jnp.einsum("rh,rd->hd", left, data, preferred_element_type=F32).astype(BF16)[None]
        for left in (d_gate, d_up, scaled_act)
    ]
    return (grad_tokens[None], grad_prob, *weight_grads)


def solution(mesh):
    in_specs = (
        P("dp", "expert", None),
        P("dp", "expert", None),
        P(None, "expert"),
        P(None, "expert"),
        P("expert", "dp", None),
        P("expert", "dp", None),
        P("expert", "dp", None),
    )
    out_specs = (
        P("dp", "expert", None),
        P("dp", "expert"),
        P("expert", "dp", None),
        P("expert", "dp", None),
        P("expert", "dp", None),
    )
    return jax.shard_map(body, mesh=mesh, in_specs=in_specs, out_specs=out_specs, check_vma=False)
```

```python
import math

import jax
import jax.numpy as jnp
from jax import lax
from jax.experimental import pallas as pl
from jax.experimental.pallas import tpu as pltpu
from jax.sharding import Mesh
from jax.sharding import PartitionSpec as P

HALF_AXES = ("dp", "low")
ALL_AXES = ("dp", "low", "top")
LANES = 128
F32, BF16 = jnp.float32, jnp.bfloat16
VMEM = pl.BlockSpec(memory_space=pltpu.VMEM)
HBM = pl.BlockSpec(memory_space=pltpu.HBM)


def dot(a, b, dims):
    return lax.dot_general(a, b, ((dims[:1], dims[1:]), ((), ())), preferred_element_type=F32)


def square(size):
    return tuple(lax.broadcasted_iota(jnp.int32, (size, size), axis) for axis in (0, 1))


def join_kernel(route_hbm, prob_hbm, tok_hbm, cot_hbm, out_ref, route_v, prob_v, sems):
    tok_dev, features = tok_hbm.shape
    small = [
        pltpu.make_async_copy(route_hbm, route_v, sems.at[0]),
        pltpu.make_async_copy(prob_hbm, prob_v, sems.at[1]),
    ]
    large = [
        pltpu.make_async_copy(tok_hbm, out_ref.at[pl.ds(0, tok_dev), pl.ds(0, features)], sems.at[2]),
        pltpu.make_async_copy(cot_hbm, out_ref.at[pl.ds(tok_dev, tok_dev), pl.ds(0, features)], sems.at[3]),
    ]
    for copy in small + large:
        copy.start()
    own = lax.broadcasted_iota(jnp.int32, route_v.shape, 0) == lax.axis_index("dp")
    here, there = square(tok_dev)
    for copy in small:
        copy.wait()
    route = jnp.sum(jnp.where(own, route_v[...].astype(F32), 0.0), axis=0, keepdims=True)
    prob = jnp.sum(jnp.where(own, prob_v[...].astype(F32), 0.0), axis=0, keepdims=True)
    route = jnp.sum(jnp.where(here == there, route, 0.0), axis=1, keepdims=True)
    prob = jnp.sum(jnp.where(here == there, prob, 0.0), axis=1, keepdims=True)
    lane = lax.broadcasted_iota(jnp.int32, (tok_dev, LANES), 1)
    tail = jnp.where(lane == 0, prob, jnp.where(lane == 1, route, 0.0))
    out_ref[:tok_dev, features:] = tail.astype(BF16)
    out_ref[tok_dev:, features:] = jnp.zeros((tok_dev, LANES), BF16)
    for copy in large:
        copy.wait()


def slots_of(rows_ref, tok_dev, features, half):
    here, there = square(tok_dev)
    column = rows_ref[:tok_dev, features + 1 : features + 2].astype(F32)
    row = jnp.sum(jnp.where(here == there, column, 0.0), axis=0, keepdims=True)
    rank = jnp.sum(jnp.where((column == row) & (here < there), 1.0, 0.0), axis=0, keepdims=True)
    route, rank = row.astype(jnp.int32), rank.astype(jnp.int32)
    upper = (route >= half).astype(jnp.int32)
    return upper, route - half * upper, rank


def pack_kernel(slots, own_ref, other_ref, gate_hbm, up_hbm, send_ref, pick_ref, gate_ref, up_ref, sems):
    copies = [
        pltpu.make_async_copy(gate_hbm, gate_ref, sems.at[0]),
        pltpu.make_async_copy(up_hbm, up_ref, sems.at[1]),
    ]
    for copy in copies:
        copy.start()
    tok_dev = own_ref.shape[0] // 2
    features = own_ref.shape[1] - LANES
    block = pick_ref.shape[0]
    groups = send_ref.shape[0] // block
    half = block // (4 * slots)
    top = lax.axis_index("top")
    place = lax.broadcasted_iota(jnp.int32, (block, tok_dev), 0)
    sent = jnp.zeros((block, features + LANES), F32)
    for rows_ref, origin in ((own_ref, top), (other_ref, 1 - top)):
        upper, low, rank = slots_of(rows_ref, tok_dev, features, half)
        target = low * (4 * slots) + origin * (2 * slots) + rank
        target = jnp.where(upper == top, target, -2 * slots)
        pick = [(place == target + shift).astype(F32) for shift in (0, slots)]
        sent += dot(jnp.concatenate(pick, axis=1).astype(BF16), rows_ref[...], (1, 0))
        if rows_ref is own_ref:
            target = (low * 2 + upper) * (2 * slots) + rank
            pick = [(place == target + shift).astype(F32) for shift in (0, slots)]
            pick_ref[...] = jnp.concatenate(pick, axis=1).astype(BF16)
    sent = sent.astype(BF16)
    for g in range(groups):
        send_ref[g * block : (g + 1) * block, :] = sent
    for copy in copies:
        copy.wait()


def expert_kernel(slots, chunk, got_ref, gate_ref, up_ref, down_hbm, *refs):
    reply_ref, dg_ref, du_ref, sa_ref, down_ref, sem = refs
    down_copy = pltpu.make_async_copy(down_hbm, down_ref, sem)
    down_copy.start()
    features = gate_ref.shape[1]
    half = features // 2

    @pl.loop(0, got_ref.shape[0] // chunk)
    def _(step):
        at = pl.ds(pl.multiple_of(step * chunk, chunk), chunk)
        data = got_ref[at, :features]
        weight = got_ref[at, features : features + 1].astype(F32)
        gate_pre = dot(data, gate_ref[...], (1, 1))
        up_pre = dot(data, up_ref[...], (1, 1))

        @pl.when(step == 0)
        def _():
            down_copy.wait()

        back_proj = dot(data, down_ref[...], (1, 1))
        back_proj = pltpu.roll(back_proj, chunk - slots, 0)
        sigma = jax.nn.sigmoid(gate_pre)
        swish = gate_pre * sigma
        slope = sigma * (1.0 + gate_pre * (1.0 - sigma))
        active = swish * up_pre
        scaled = weight * active
        d_active = weight * back_proj
        d_gate = d_active * up_pre * slope
        d_up = d_active * swish
        part = jnp.sum(active * back_proj, axis=1, keepdims=True)
        dg, dg_low = d_gate.astype(BF16), pltpu.roll(d_gate, slots, 0).astype(BF16)
        du, du_low = d_up.astype(BF16), pltpu.roll(d_up, slots, 0).astype(BF16)
        dg_ref[at, :] = dg
        du_ref[at, :] = du
        sa_ref[at, :] = pltpu.roll(scaled, slots, 0).astype(BF16)
        grad = dot(dg, gate_ref[:, :half], (1, 0)) + dot(du, up_ref[:, :half], (1, 0))
        grad += dot(dg_low, gate_ref[:, half:], (1, 0)) + dot(du_low, up_ref[:, half:], (1, 0))
        reply_ref[at, :half] = grad.astype(BF16)
        reply_ref[at, half:] = jnp.broadcast_to(part, (chunk, LANES)).astype(BF16)


def unpack_kernel(pick_ref, back_ref, tok_ref, prob_ref):
    tok_dev, features = tok_ref.shape
    half = features // 2
    total = dot(pick_ref[...], back_ref[...], (1, 0))
    tok_ref[:, :half] = total[:tok_dev, :half].astype(BF16)
    tok_ref[:, half:] = total[tok_dev:, :half].astype(BF16)
    part = total[:tok_dev, half:]
    here = lax.broadcasted_iota(jnp.int32, part.shape, 0)
    diagonal = here == lax.broadcasted_iota(jnp.int32, part.shape, 1)
    part = jnp.sum(jnp.where(diagonal, part, 0.0), axis=0, keepdims=True)
    prob_ref[...] = part[:, :tok_dev]


def near(shape, dtype=BF16):
    small = shape[0] * shape[1] <= 1 << 20
    return pltpu.VMEM(shape, dtype) if small else jax.ShapeDtypeStruct(shape, dtype)


def fetched(array):
    small = array.size <= 1 << 20
    return pltpu.with_memory_space_constraint(array, pltpu.VMEM) if small else array


def far(*arrays):
    return [pltpu.with_memory_space_constraint(a, pltpu.HBM) for a in arrays]


def call(kernel, in_specs, outs, *args, scratch=()):
    return pl.pallas_call(
        kernel,
        in_specs=in_specs,
        scratch_shapes=scratch,
        out_specs=[VMEM] * len(outs),
        out_shape=outs,
        compiler_params=pltpu.CompilerParams(vmem_limit_bytes=(16 if all(math.prod(o.shape) <= 1 << 20 for o in outs) else 48) << 20),
    )(*args)


def body(tokens, cotangent, routes, gate_prob, w_gate, w_up, w_down):
    groups = lax.axis_size("dp")
    experts = 2 * lax.axis_size("low")
    _, tok_dev, features = tokens.shape
    hidden = w_gate.shape[1]
    half = features // 2
    slots = tok_dev // 4
    block = experts * 2 * slots
    rows = groups * block
    chunk = min(rows, 256)
    width = features + LANES

    (own,) = call(
        join_kernel,
        [HBM] * 4,
        [near((2 * tok_dev, width))],
        *far(routes, gate_prob, tokens[0], cotangent[0]),
        scratch=[
            pltpu.VMEM(routes.shape, routes.dtype),
            pltpu.VMEM(gate_prob.shape, gate_prob.dtype),
            pltpu.SemaphoreType.DMA((4,)),
        ],
    )
    other = lax.ppermute(own, "top", [(0, 1), (1, 0)])
    send, pick, gate_near, up_near = call(
        lambda *refs: pack_kernel(slots, *refs),
        [VMEM] * 2 + [HBM] * 2,
        [near((rows, width)), near((block, 2 * tok_dev))] + [near((hidden, features))] * 2,
        fetched(own), fetched(other), *far(w_gate[0], w_up[0]),
        scratch=[pltpu.SemaphoreType.DMA((2,))],
    )
    got = lax.all_to_all(send, HALF_AXES, split_axis=0, concat_axis=0, tiled=True)
    reply, d_gate, d_up, scaled_act = call(
        lambda *refs: expert_kernel(slots, chunk, *refs),
        [VMEM] * 3 + [HBM],
        [near((rows, half + LANES))] + [near((rows, hidden))] * 3,
        fetched(got), fetched(gate_near), fetched(up_near), *far(w_down[0]),
        scratch=[pltpu.VMEM((hidden, features), BF16), pltpu.SemaphoreType.DMA(())],
    )
    back = lax.all_to_all(reply, ALL_AXES, split_axis=0, concat_axis=0, tiled=True)
    grad_tokens, grad_prob = call(
        unpack_kernel,
        [VMEM] * 2,
        [jax.ShapeDtypeStruct((tok_dev, features), BF16), jax.ShapeDtypeStruct((1, tok_dev), F32)],
        jnp.tile(pick.T, (1, groups)), back,
    )
    data = got[:, :features]
    weight_grads = [
        jnp.einsum("rh,rd->hd", left, data, preferred_element_type=F32).astype(BF16)[None]
        for left in (d_gate, d_up, scaled_act)
    ]
    return (grad_tokens[None], grad_prob, *weight_grads)


def solution(mesh):
    groups, experts = (mesh.shape[axis] for axis in ("dp", "expert"))
    split = Mesh(mesh.devices.reshape(groups, 2, experts // 2), ("dp", "top", "low"))
    expert = ("top", "low")
    in_specs = (
        P("dp", expert, None),
        P("dp", expert, None),
        P(None, expert),
        P(None, expert),
        P(expert, "dp", None),
        P(expert, "dp", None),
        P(expert, "dp", None),
    )
    out_specs = (
        P("dp", expert, None),
        P("dp", expert),
        P(expert, "dp", None),
        P(expert, "dp", None),
        P(expert, "dp", None),
    )
    return jax.shard_map(body, mesh=split, in_specs=in_specs, out_specs=out_specs, check_vma=False)
```

```python
import math

import jax
import jax.numpy as jnp
from jax import lax
from jax.experimental import pallas as pl
from jax.experimental.pallas import tpu as pltpu
from jax.sharding import Mesh
from jax.sharding import PartitionSpec as P

HALF_AXES = ("dp", "low")
ALL_AXES = ("dp", "low", "top")
LANES = 128
F32, BF16 = jnp.float32, jnp.bfloat16
VMEM = pl.BlockSpec(memory_space=pltpu.VMEM)
HBM = pl.BlockSpec(memory_space=pltpu.HBM)


def dot(a, b, dims):
    return lax.dot_general(a, b, ((dims[:1], dims[1:]), ((), ())), preferred_element_type=F32)


def square(size):
    return tuple(lax.broadcasted_iota(jnp.int32, (size, size), axis) for axis in (0, 1))


def join_kernel(route_hbm, prob_hbm, tok_hbm, cot_hbm, out_ref, route_v, prob_v, sems):
    tok_dev, features = tok_hbm.shape
    small = [
        pltpu.make_async_copy(route_hbm, route_v, sems.at[0]),
        pltpu.make_async_copy(prob_hbm, prob_v, sems.at[1]),
    ]
    large = [
        pltpu.make_async_copy(tok_hbm, out_ref.at[pl.ds(0, tok_dev), pl.ds(0, features)], sems.at[2]),
        pltpu.make_async_copy(cot_hbm, out_ref.at[pl.ds(tok_dev, tok_dev), pl.ds(0, features)], sems.at[3]),
    ]
    for copy in small + large:
        copy.start()
    own = lax.broadcasted_iota(jnp.int32, route_v.shape, 0) == lax.axis_index("dp")
    here, there = square(tok_dev)
    for copy in small:
        copy.wait()
    route = jnp.sum(jnp.where(own, route_v[...].astype(F32), 0.0), axis=0, keepdims=True)
    prob = jnp.sum(jnp.where(own, prob_v[...].astype(F32), 0.0), axis=0, keepdims=True)
    route = jnp.sum(jnp.where(here == there, route, 0.0), axis=1, keepdims=True)
    prob = jnp.sum(jnp.where(here == there, prob, 0.0), axis=1, keepdims=True)
    lane = lax.broadcasted_iota(jnp.int32, (tok_dev, LANES), 1)
    tail = jnp.where(lane == 0, prob, jnp.where(lane == 1, route, 0.0))
    out_ref[:tok_dev, features:] = tail.astype(BF16)
    out_ref[tok_dev:, features:] = jnp.zeros((tok_dev, LANES), BF16)
    for copy in large:
        copy.wait()


def slots_of(rows_ref, tok_dev, features, half):
    here, there = square(tok_dev)
    column = rows_ref[:tok_dev, features + 1 : features + 2].astype(F32)
    row = jnp.sum(jnp.where(here == there, column, 0.0), axis=0, keepdims=True)
    rank = jnp.sum(jnp.where((column == row) & (here < there), 1.0, 0.0), axis=0, keepdims=True)
    route, rank = row.astype(jnp.int32), rank.astype(jnp.int32)
    upper = (route >= half).astype(jnp.int32)
    return upper, route - half * upper, rank


def load_kernel(*refs):
    ins, outs, sems = refs[:3], refs[3:6], refs[6]
    copies = [pltpu.make_async_copy(a, b, sems.at[i]) for i, (a, b) in enumerate(zip(ins, outs))]
    for copy in copies:
        copy.start()
    for copy in copies:
        copy.wait()


def pack_kernel(slots, own_ref, other_ref, w0, w1, w2, send_ref, pick_ref):
    del w0, w1, w2
    tok_dev = own_ref.shape[0] // 2
    features = own_ref.shape[1] - LANES
    block = pick_ref.shape[0]
    groups = send_ref.shape[0] // block
    half = block // (4 * slots)
    top = lax.axis_index("top")
    place = lax.broadcasted_iota(jnp.int32, (block, tok_dev), 0)
    sent = jnp.zeros((block, features + LANES), F32)
    for rows_ref, origin in ((own_ref, top), (other_ref, 1 - top)):
        upper, low, rank = slots_of(rows_ref, tok_dev, features, half)
        target = low * (4 * slots) + origin * (2 * slots) + rank
        target = jnp.where(upper == top, target, -2 * slots)
        pick = [(place == target + shift).astype(F32) for shift in (0, slots)]
        sent += dot(jnp.concatenate(pick, axis=1).astype(BF16), rows_ref[...], (1, 0))
        if rows_ref is own_ref:
            target = (low * 2 + upper) * (2 * slots) + rank
            pick = [(place == target + shift).astype(F32) for shift in (0, slots)]
            pick_ref[...] = jnp.concatenate(pick, axis=1).astype(BF16)
    sent = sent.astype(BF16)
    for g in range(groups):
        send_ref[g * block : (g + 1) * block, :] = sent


def expert_kernel(slots, chunk, got_ref, gate_ref, up_ref, down_ref, *refs):
    reply_ref, dg_ref, du_ref, sa_ref = refs
    features = gate_ref.shape[1]
    half = features // 2

    @pl.loop(0, got_ref.shape[0] // chunk)
    def _(step):
        at = pl.ds(pl.multiple_of(step * chunk, chunk), chunk)
        data = got_ref[at, :features]
        weight = got_ref[at, features : features + 1].astype(F32)
        gate_pre = dot(data, gate_ref[...], (1, 1))
        up_pre = dot(data, up_ref[...], (1, 1))
        back_proj = dot(data, down_ref[...], (1, 1))
        back_proj = pltpu.roll(back_proj, chunk - slots, 0)
        sigma = jax.nn.sigmoid(gate_pre)
        swish = gate_pre * sigma
        slope = sigma * (1.0 + gate_pre * (1.0 - sigma))
        active = swish * up_pre
        scaled = weight * active
        d_active = weight * back_proj
        d_gate = d_active * up_pre * slope
        d_up = d_active * swish
        part = jnp.sum(active * back_proj, axis=1, keepdims=True)
        dg, dg_low = d_gate.astype(BF16), pltpu.roll(d_gate, slots, 0).astype(BF16)
        du, du_low = d_up.astype(BF16), pltpu.roll(d_up, slots, 0).astype(BF16)
        dg_ref[at, :] = dg
        du_ref[at, :] = du
        sa_ref[at, :] = pltpu.roll(scaled, slots, 0).astype(BF16)
        grad = dot(dg, gate_ref[:, :half], (1, 0)) + dot(du, up_ref[:, :half], (1, 0))
        grad += dot(dg_low, gate_ref[:, half:], (1, 0)) + dot(du_low, up_ref[:, half:], (1, 0))
        reply_ref[at, :half] = grad.astype(BF16)
        reply_ref[at, half:] = jnp.broadcast_to(part, (chunk, LANES)).astype(BF16)


def unpack_kernel(pick_ref, back_ref, tok_ref, prob_ref):
    tok_dev, features = tok_ref.shape
    half = features // 2
    total = dot(pick_ref[...], back_ref[...], (1, 0))
    tok_ref[:, :half] = total[:tok_dev, :half].astype(BF16)
    tok_ref[:, half:] = total[tok_dev:, :half].astype(BF16)
    part = total[:tok_dev, half:]
    here = lax.broadcasted_iota(jnp.int32, part.shape, 0)
    diagonal = here == lax.broadcasted_iota(jnp.int32, part.shape, 1)
    part = jnp.sum(jnp.where(diagonal, part, 0.0), axis=0, keepdims=True)
    prob_ref[...] = part[:, :tok_dev]


def near(shape, dtype=BF16):
    small = shape[0] * shape[1] <= 1 << 20
    return pltpu.VMEM(shape, dtype) if small else jax.ShapeDtypeStruct(shape, dtype)


def fetched(array):
    small = array.size <= 1 << 20
    return pltpu.with_memory_space_constraint(array, pltpu.VMEM) if small else array


def far(*arrays):
    return [pltpu.with_memory_space_constraint(a, pltpu.HBM) for a in arrays]


def call(kernel, in_specs, outs, *args, scratch=(), cost=None):
    return pl.pallas_call(
        kernel,
        in_specs=in_specs,
        scratch_shapes=scratch,
        out_specs=[VMEM] * len(outs),
        out_shape=outs,
        cost_estimate=cost,
        compiler_params=pltpu.CompilerParams(vmem_limit_bytes=(16 if all(math.prod(o.shape) <= 1 << 20 for o in outs) else 48) << 20),
    )(*args)


def body(tokens, cotangent, routes, gate_prob, w_gate, w_up, w_down):
    groups = lax.axis_size("dp")
    experts = 2 * lax.axis_size("low")
    _, tok_dev, features = tokens.shape
    hidden = w_gate.shape[1]
    half = features // 2
    slots = tok_dev // 4
    block = experts * 2 * slots
    rows = groups * block
    chunk = min(rows, 256)
    width = features + LANES

    (own,) = call(
        join_kernel,
        [HBM] * 4,
        [near((2 * tok_dev, width))],
        *far(routes, gate_prob, tokens[0], cotangent[0]),
        scratch=[
            pltpu.VMEM(routes.shape, routes.dtype),
            pltpu.VMEM(gate_prob.shape, gate_prob.dtype),
            pltpu.SemaphoreType.DMA((4,)),
        ],
    )
    other = lax.ppermute(own, "top", [(0, 1), (1, 0)])
    weights = call(
        load_kernel,
        [HBM] * 3,
        [near((hidden, features))] * 3,
        *far(w_gate[0], w_up[0], w_down[0]),
        scratch=[pltpu.SemaphoreType.DMA((3,))],
        cost=pl.CostEstimate(flops=0, transcendentals=0, bytes_accessed=12 * hidden * features),
    )
    weights = [fetched(a) for a in weights]
    send, pick = call(
        lambda *refs: pack_kernel(slots, *refs),
        [VMEM] * 5,
        [near((rows, width)), near((block, 2 * tok_dev))],
        fetched(own), fetched(other), *weights,
    )
    got = lax.all_to_all(send, HALF_AXES, split_axis=0, concat_axis=0, tiled=True)
    reply, d_gate, d_up, scaled_act = call(
        lambda *refs: expert_kernel(slots, chunk, *refs),
        [VMEM] * 4,
        [near((rows, half + LANES))] + [near((rows, hidden))] * 3,
        fetched(got), *weights,
    )
    back = lax.all_to_all(reply, ALL_AXES, split_axis=0, concat_axis=0, tiled=True)
    grad_tokens, grad_prob = call(
        unpack_kernel,
        [VMEM] * 2,
        [jax.ShapeDtypeStruct((tok_dev, features), BF16), jax.ShapeDtypeStruct((1, tok_dev), F32)],
        jnp.tile(pick.T, (1, groups)), back,
    )
    data = got[:, :features]
    weight_grads = [
        jnp.einsum("rh,rd->hd", left, data, preferred_element_type=F32).astype(BF16)[None]
        for left in (d_gate, d_up, scaled_act)
    ]
    return (grad_tokens[None], grad_prob, *weight_grads)


def solution(mesh):
    groups, experts = (mesh.shape[axis] for axis in ("dp", "expert"))
    split = Mesh(mesh.devices.reshape(groups, 2, experts // 2), ("dp", "top", "low"))
    expert = ("top", "low")
    in_specs = (
        P("dp", expert, None),
        P("dp", expert, None),
        P(None, expert),
        P(None, expert),
        P(expert, "dp", None),
        P(expert, "dp", None),
        P(expert, "dp", None),
    )
    out_specs = (
        P("dp", expert, None),
        P("dp", expert),
        P(expert, "dp", None),
        P(expert, "dp", None),
        P(expert, "dp", None),
    )
    return jax.shard_map(body, mesh=split, in_specs=in_specs, out_specs=out_specs, check_vma=False)
```

```python
import math

import jax
import jax.numpy as jnp
from jax import lax
from jax.experimental import pallas as pl
from jax.experimental.pallas import tpu as pltpu
from jax.sharding import Mesh
from jax.sharding import PartitionSpec as P

HALF_AXES = ("dp", "low")
SWAP = [(0, 1), (1, 0)]
LANES = 128
NEAR_SIZE = 1 << 20
F32, BF16 = jnp.float32, jnp.bfloat16
VMEM = pl.BlockSpec(memory_space=pltpu.VMEM)
HBM = pl.BlockSpec(memory_space=pltpu.HBM)


def dot(a, b, dims):
    return lax.dot_general(a, b, ((dims[:1], dims[1:]), ((), ())), preferred_element_type=F32)


def square(size):
    return tuple(lax.broadcasted_iota(jnp.int32, (size, size), axis) for axis in (0, 1))


def join_kernel(route_hbm, prob_hbm, tok_hbm, cot_hbm, out_ref, route_v, prob_v, sems):
    tok_dev, features = tok_hbm.shape
    small = [
        pltpu.make_async_copy(route_hbm, route_v, sems.at[0]),
        pltpu.make_async_copy(prob_hbm, prob_v, sems.at[1]),
    ]
    large = [
        pltpu.make_async_copy(tok_hbm, out_ref.at[:, pl.ds(0, features)], sems.at[2]),
        pltpu.make_async_copy(cot_hbm, out_ref.at[:, pl.ds(features, features)], sems.at[3]),
    ]
    for copy in small + large:
        copy.start()
    own = lax.broadcasted_iota(jnp.int32, route_v.shape, 0) == lax.axis_index("dp")
    here, there = square(tok_dev)
    for copy in small:
        copy.wait()
    route = jnp.sum(jnp.where(own, route_v[...].astype(F32), 0.0), axis=0, keepdims=True)
    prob = jnp.sum(jnp.where(own, prob_v[...].astype(F32), 0.0), axis=0, keepdims=True)
    route = jnp.sum(jnp.where(here == there, route, 0.0), axis=1, keepdims=True)
    prob = jnp.sum(jnp.where(here == there, prob, 0.0), axis=1, keepdims=True)
    lane = lax.broadcasted_iota(jnp.int32, (tok_dev, LANES), 1)
    tail = jnp.where(lane == 0, prob, jnp.where(lane == 1, route, 0.0))
    out_ref[:, 2 * features :] = tail.astype(BF16)
    for copy in large:
        copy.wait()


def load_kernel(*refs):
    ins, outs, sems = refs[:3], refs[3:6], refs[6]
    copies = [pltpu.make_async_copy(a, b, sems.at[i]) for i, (a, b) in enumerate(zip(ins, outs))]
    for copy in copies:
        copy.start()
    for copy in copies:
        copy.wait()


def pack_kernel(slots, own_ref, other_ref, w0, w1, w2, send_ref, pick_ref):
    del w0, w1, w2
    tok_dev, width = own_ref.shape
    block = pick_ref.shape[0]
    groups = send_ref.shape[0] // block
    half = block // (2 * slots)
    top = lax.axis_index("top")
    here, there = square(tok_dev)
    place = lax.broadcasted_iota(jnp.int32, (block, tok_dev), 0)
    sent = jnp.zeros((block, width), F32)
    picks = []
    for rows_ref, origin in ((own_ref, top), (other_ref, 1 - top)):
        column = rows_ref[:, width - LANES + 1 : width - LANES + 2].astype(F32)
        row = jnp.sum(jnp.where(here == there, column, 0.0), axis=0, keepdims=True)
        rank = jnp.sum(jnp.where((column == row) & (here < there), 1.0, 0.0), axis=0, keepdims=True)
        low = row.astype(jnp.int32) - top * half
        target = low * (2 * slots) + origin * slots + rank.astype(jnp.int32)
        target = jnp.where((low >= 0) & (low < half), target, -1)
        pick = (place == target).astype(F32).astype(BF16)
        sent += dot(pick, rows_ref[...], (1, 0))
        picks.append(pick)
    pick_ref[:, :tok_dev] = picks[0]
    pick_ref[:, tok_dev:] = picks[1]
    sent = sent.astype(BF16)
    for g in range(groups):
        send_ref[g * block : (g + 1) * block, :] = sent


def expert_kernel(chunk, got_ref, gate_ref, up_ref, down_ref, reply_ref, dg_ref, du_ref, sa_ref):
    features = gate_ref.shape[1]
    mine = lax.axis_index("dp")
    lane = lax.broadcasted_iota(jnp.int32, (chunk, LANES), 1)

    @pl.loop(0, got_ref.shape[0] // chunk)
    def _(step):
        at = pl.ds(pl.multiple_of(step * chunk, chunk), chunk)
        rows_x = got_ref[at, :features]
        rows_dy = got_ref[at, features : 2 * features]
        weight = got_ref[at, 2 * features : 2 * features + 1].astype(F32)
        gate_pre = dot(rows_x, gate_ref[...], (1, 1))
        up_pre = dot(rows_x, up_ref[...], (1, 1))
        back_proj = dot(rows_dy, down_ref[...], (1, 1))
        sigma = jax.nn.sigmoid(gate_pre)
        swish = gate_pre * sigma
        slope = sigma * (1.0 + gate_pre * (1.0 - sigma))
        active = swish * up_pre
        d_active = weight * back_proj
        d_gate = (d_active * up_pre * slope).astype(BF16)
        d_up = (d_active * swish).astype(BF16)
        part = jnp.sum(active * back_proj, axis=1, keepdims=True)
        dg_ref[at, :] = d_gate
        du_ref[at, :] = d_up
        sa_ref[at, :] = (weight * active).astype(BF16)
        grad = dot(d_gate, gate_ref[...], (1, 0)) + dot(d_up, up_ref[...], (1, 0))
        reply_ref[at, :features] = grad.astype(BF16)
        reply_ref[at, features:] = jnp.where(lane == mine, part, 0.0).astype(BF16)


def combine_kernel(pick_ref, back_ref, own_ref, other_ref):
    total = dot(pick_ref[...], back_ref[...], (1, 0)).astype(BF16)
    own_ref[...] = total[: own_ref.shape[0]]
    other_ref[...] = total[own_ref.shape[0] :]


def finish_kernel(own_ref, other_ref, tok_ref, prob_ref):
    tok_dev, features = tok_ref.shape
    total = own_ref[...].astype(F32) + other_ref[...].astype(F32)
    tok_ref[...] = total[:, :features].astype(BF16)
    part = jnp.sum(total[:, features:], axis=1, keepdims=True)
    here, there = square(tok_dev)
    prob_ref[...] = jnp.sum(jnp.where(here == there, part, 0.0), axis=0, keepdims=True)


def near(shape, dtype=BF16):
    small = math.prod(shape) <= NEAR_SIZE
    return pltpu.VMEM(shape, dtype) if small else jax.ShapeDtypeStruct(shape, dtype)


def fetched(array):
    small = array.size <= NEAR_SIZE
    return pltpu.with_memory_space_constraint(array, pltpu.VMEM) if small else array


def far(*arrays):
    return [pltpu.with_memory_space_constraint(a, pltpu.HBM) for a in arrays]


def call(kernel, in_specs, outs, *args, scratch=(), cost=None):
    small = all(math.prod(out.shape) <= NEAR_SIZE for out in outs)
    return pl.pallas_call(
        kernel,
        in_specs=in_specs,
        scratch_shapes=scratch,
        out_specs=[VMEM] * len(outs),
        out_shape=outs,
        cost_estimate=cost,
        compiler_params=pltpu.CompilerParams(vmem_limit_bytes=(16 if small else 48) << 20),
    )(*args)


def body(tokens, cotangent, routes, gate_prob, w_gate, w_up, w_down):
    groups = lax.axis_size("dp")
    half = lax.axis_size("low")
    _, tok_dev, features = tokens.shape
    hidden = w_gate.shape[1]
    slots = tok_dev // 4
    block = half * 2 * slots
    rows = groups * block
    chunk = min(rows, 256)
    width = 2 * features + LANES

    (own,) = call(
        join_kernel,
        [HBM] * 4,
        [near((tok_dev, width))],
        *far(routes, gate_prob, tokens[0], cotangent[0]),
        scratch=[
            pltpu.VMEM(routes.shape, routes.dtype),
            pltpu.VMEM(gate_prob.shape, gate_prob.dtype),
            pltpu.SemaphoreType.DMA((4,)),
        ],
    )
    other = lax.ppermute(own, "top", SWAP)
    weights = call(
        load_kernel,
        [HBM] * 3,
        [near((hidden, features))] * 3,
        *far(w_gate[0], w_up[0], w_down[0]),
        scratch=[pltpu.SemaphoreType.DMA((3,))],
        cost=pl.CostEstimate(flops=0, transcendentals=0, bytes_accessed=12 * hidden * features),
    )
    weights = [fetched(a) for a in weights]
    send, pick = call(
        lambda *refs: pack_kernel(slots, *refs),
        [VMEM] * 5,
        [near((rows, width)), near((block, 2 * tok_dev))],
        fetched(own), fetched(other), *weights,
    )
    got = lax.all_to_all(send, HALF_AXES, split_axis=0, concat_axis=0, tiled=True)
    reply, d_gate, d_up, scaled_act = call(
        lambda *refs: expert_kernel(chunk, *refs),
        [VMEM] * 4,
        [near((rows, features + LANES))] + [near((rows, hidden))] * 3,
        fetched(got), *weights,
    )
    back = lax.all_to_all(reply, HALF_AXES, split_axis=0, concat_axis=0, tiled=True)
    kept, given = call(
        combine_kernel,
        [VMEM] * 2,
        [near((tok_dev, features + LANES))] * 2,
        jnp.tile(pick.T, (1, groups)), back,
    )
    grad_tokens, grad_prob = call(
        finish_kernel,
        [VMEM] * 2,
        [jax.ShapeDtypeStruct((tok_dev, features), BF16), jax.ShapeDtypeStruct((1, tok_dev), F32)],
        fetched(kept), fetched(lax.ppermute(given, "top", SWAP)),
    )
    rows_x, rows_dy = got[:, :features], got[:, features : 2 * features]
    weight_grads = [
        jnp.einsum("rh,rd->hd", left, right, preferred_element_type=F32).astype(BF16)[None]
        for left, right in ((d_gate, rows_x), (d_up, rows_x), (scaled_act, rows_dy))
    ]
    return (grad_tokens[None], grad_prob, *weight_grads)


def solution(mesh):
    groups, experts = (mesh.shape[axis] for axis in ("dp", "expert"))
    split = Mesh(mesh.devices.reshape(groups, 2, experts // 2), ("dp", "top", "low"))
    expert = ("top", "low")
    in_specs = (
        P("dp", expert, None),
        P("dp", expert, None),
        P(None, expert),
        P(None, expert),
        P(expert, "dp", None),
        P(expert, "dp", None),
        P(expert, "dp", None),
    )
    out_specs = (
        P("dp", expert, None),
        P("dp", expert),
        P(expert, "dp", None),
        P(expert, "dp", None),
        P(expert, "dp", None),
    )
    return jax.shard_map(body, mesh=split, in_specs=in_specs, out_specs=out_specs, check_vma=False)
```

```python
import math

import jax
import jax.numpy as jnp
from jax import lax
from jax.experimental import pallas as pl
from jax.experimental.pallas import tpu as pltpu
from jax.sharding import Mesh
from jax.sharding import PartitionSpec as P

HALF_AXES = ("dp", "low")
SWAP = [(0, 1), (1, 0)]
LANES = 128
NEAR_SIZE = 2 << 20
F32, BF16 = jnp.float32, jnp.bfloat16
VMEM = pl.BlockSpec(memory_space=pltpu.VMEM)
HBM = pl.BlockSpec(memory_space=pltpu.HBM)


def dot(a, b, dims):
    return lax.dot_general(a, b, ((dims[:1], dims[1:]), ((), ())), preferred_element_type=F32)


def square(size):
    return tuple(lax.broadcasted_iota(jnp.int32, (size, size), axis) for axis in (0, 1))


def join_kernel(route_hbm, prob_hbm, tok_hbm, cot_hbm, out_ref, route_v, prob_v, sems):
    tok_dev, features = tok_hbm.shape
    small = [
        pltpu.make_async_copy(route_hbm, route_v, sems.at[0]),
        pltpu.make_async_copy(prob_hbm, prob_v, sems.at[1]),
    ]
    large = [
        pltpu.make_async_copy(tok_hbm, out_ref.at[:, pl.ds(0, features)], sems.at[2]),
        pltpu.make_async_copy(cot_hbm, out_ref.at[:, pl.ds(features, features)], sems.at[3]),
    ]
    for copy in small + large:
        copy.start()
    own = lax.broadcasted_iota(jnp.int32, route_v.shape, 0) == lax.axis_index("dp")
    here, there = square(tok_dev)
    for copy in small:
        copy.wait()
    route = jnp.sum(jnp.where(own, route_v[...].astype(F32), 0.0), axis=0, keepdims=True)
    prob = jnp.sum(jnp.where(own, prob_v[...].astype(F32), 0.0), axis=0, keepdims=True)
    route = jnp.sum(jnp.where(here == there, route, 0.0), axis=1, keepdims=True)
    prob = jnp.sum(jnp.where(here == there, prob, 0.0), axis=1, keepdims=True)
    lane = lax.broadcasted_iota(jnp.int32, (tok_dev, LANES), 1)
    tail = jnp.where(lane == 0, prob, jnp.where(lane == 1, route, 0.0))
    out_ref[:, 2 * features :] = tail.astype(BF16)
    for copy in large:
        copy.wait()


def load_kernel(gate_hbm, up_hbm, down_hbm, rows_ref, gate_t, up_t, down_t, down_v, sems):
    hidden = gate_hbm.shape[0]
    places = (rows_ref.at[pl.ds(0, hidden), :], rows_ref.at[pl.ds(hidden, hidden), :], down_v)
    copies = [
        pltpu.make_async_copy(a, b, sems.at[i])
        for i, (a, b) in enumerate(zip((gate_hbm, up_hbm, down_hbm), places))
    ]
    for copy in copies:
        copy.start()
    for copy, place, turned in zip(copies, places, (gate_t, up_t, down_t)):
        copy.wait()
        turned[...] = place[...].T


def pack_kernel(slots, own_ref, other_ref, w0, w1, w2, w3, send_ref, pick_ref):
    del w0, w1, w2, w3
    tok_dev, width = own_ref.shape
    block = pick_ref.shape[0]
    groups = send_ref.shape[0] // block
    half = block // (2 * slots)
    top = lax.axis_index("top")
    here, there = square(tok_dev)
    place = lax.broadcasted_iota(jnp.int32, (block, tok_dev), 0)
    sent = jnp.zeros((block, width), F32)
    picks = []
    for rows_ref, origin in ((own_ref, top), (other_ref, 1 - top)):
        column = rows_ref[:, width - LANES + 1 : width - LANES + 2].astype(F32)
        row = jnp.sum(jnp.where(here == there, column, 0.0), axis=0, keepdims=True)
        rank = jnp.sum(jnp.where((column == row) & (here < there), 1.0, 0.0), axis=0, keepdims=True)
        low = row.astype(jnp.int32) - top * half
        target = low * (2 * slots) + origin * slots + rank.astype(jnp.int32)
        target = jnp.where((low >= 0) & (low < half), target, -1)
        pick = (place == target).astype(F32).astype(BF16)
        sent += dot(pick, rows_ref[...], (1, 0))
        picks.append(pick)
    pick_ref[:, :tok_dev] = picks[0]
    pick_ref[:, tok_dev:] = picks[1]
    sent = sent.astype(BF16)
    for g in range(groups):
        send_ref[g * block : (g + 1) * block, :] = sent


def expert_kernel(chunk, got_ref, rows_ref, gate_t, up_t, down_t, reply_ref, dg_ref, du_ref, sa_ref):
    features = rows_ref.shape[1]
    mine = lax.axis_index("dp")
    lane = lax.broadcasted_iota(jnp.int32, (chunk, LANES), 1)

    @pl.loop(0, got_ref.shape[0] // chunk)
    def _(step):
        at = pl.ds(pl.multiple_of(step * chunk, chunk), chunk)
        rows_x = got_ref[at, :features]
        rows_dy = got_ref[at, features : 2 * features]
        weight = got_ref[at, 2 * features : 2 * features + 1].astype(F32)
        gate_pre = dot(rows_x, gate_t[...], (1, 0))
        up_pre = dot(rows_x, up_t[...], (1, 0))
        back_proj = dot(rows_dy, down_t[...], (1, 0))
        sigma = jax.nn.sigmoid(gate_pre)
        swish = gate_pre * sigma
        slope = sigma * (1.0 + gate_pre * (1.0 - sigma))
        active = swish * up_pre
        d_active = weight * back_proj
        d_gate = (d_active * up_pre * slope).astype(BF16)
        d_up = (d_active * swish).astype(BF16)
        part = jnp.sum(active * back_proj, axis=1, keepdims=True)
        dg_ref[at, :] = d_gate
        du_ref[at, :] = d_up
        sa_ref[at, :] = (weight * active).astype(BF16)
        grad = dot(jnp.concatenate([d_gate, d_up], axis=1), rows_ref[...], (1, 0))
        reply_ref[at, :features] = grad.astype(BF16)
        reply_ref[at, features:] = jnp.where(lane == mine, part, 0.0).astype(BF16)


def combine_kernel(pick_ref, back_ref, own_ref, other_ref):
    total = dot(pick_ref[...], back_ref[...], (1, 0)).astype(BF16)
    own_ref[...] = total[: own_ref.shape[0]]
    other_ref[...] = total[own_ref.shape[0] :]


def finish_kernel(own_ref, other_ref, tok_ref, prob_ref):
    tok_dev, features = tok_ref.shape
    total = own_ref[...].astype(F32) + other_ref[...].astype(F32)
    tok_ref[...] = total[:, :features].astype(BF16)
    part = jnp.sum(total[:, features:], axis=1, keepdims=True)
    here, there = square(tok_dev)
    prob_ref[...] = jnp.sum(jnp.where(here == there, part, 0.0), axis=0, keepdims=True)


def near(shape, dtype=BF16):
    small = math.prod(shape) <= NEAR_SIZE
    return pltpu.VMEM(shape, dtype) if small else jax.ShapeDtypeStruct(shape, dtype)


def fetched(array):
    small = array.size <= NEAR_SIZE
    return pltpu.with_memory_space_constraint(array, pltpu.VMEM) if small else array


def far(*arrays):
    return [pltpu.with_memory_space_constraint(a, pltpu.HBM) for a in arrays]


def call(kernel, in_specs, outs, *args, scratch=(), cost=None):
    small = all(math.prod(out.shape) <= NEAR_SIZE for out in outs)
    return pl.pallas_call(
        kernel,
        in_specs=in_specs,
        scratch_shapes=scratch,
        out_specs=[VMEM] * len(outs),
        out_shape=outs,
        cost_estimate=cost,
        compiler_params=pltpu.CompilerParams(vmem_limit_bytes=(16 if small else 48) << 20),
    )(*args)


def body(tokens, cotangent, routes, gate_prob, w_gate, w_up, w_down):
    groups = lax.axis_size("dp")
    half = lax.axis_size("low")
    _, tok_dev, features = tokens.shape
    hidden = w_gate.shape[1]
    slots = tok_dev // 4
    block = half * 2 * slots
    rows = groups * block
    chunk = min(rows, 256)
    width = 2 * features + LANES

    (own,) = call(
        join_kernel,
        [HBM] * 4,
        [near((tok_dev, width))],
        *far(routes, gate_prob, tokens[0], cotangent[0]),
        scratch=[
            pltpu.VMEM(routes.shape, routes.dtype),
            pltpu.VMEM(gate_prob.shape, gate_prob.dtype),
            pltpu.SemaphoreType.DMA((4,)),
        ],
    )
    other = lax.ppermute(own, "top", SWAP)
    weights = call(
        load_kernel,
        [HBM] * 3,
        [near((2 * hidden, features))] + [near((features, hidden))] * 3,
        *far(w_gate[0], w_up[0], w_down[0]),
        scratch=[pltpu.VMEM((hidden, features), BF16), pltpu.SemaphoreType.DMA((3,))],
        cost=pl.CostEstimate(flops=0, transcendentals=0, bytes_accessed=16 * hidden * features),
    )
    weights = [fetched(a) for a in weights]
    send, pick = call(
        lambda *refs: pack_kernel(slots, *refs),
        [VMEM] * 6,
        [near((rows, width)), near((block, 2 * tok_dev))],
        fetched(own), fetched(other), *weights,
    )
    got = lax.all_to_all(send, HALF_AXES, split_axis=0, concat_axis=0, tiled=True)
    reply, d_gate, d_up, scaled_act = call(
        lambda *refs: expert_kernel(chunk, *refs),
        [VMEM] * 5,
        [near((rows, features + LANES))] + [near((rows, hidden))] * 3,
        fetched(got), *weights,
    )
    back = lax.all_to_all(reply, HALF_AXES, split_axis=0, concat_axis=0, tiled=True)
    kept, given = call(
        combine_kernel,
        [VMEM] * 2,
        [near((tok_dev, features + LANES))] * 2,
        jnp.tile(pick.T, (1, groups)), back,
    )
    grad_tokens, grad_prob = call(
        finish_kernel,
        [VMEM] * 2,
        [jax.ShapeDtypeStruct((tok_dev, features), BF16), jax.ShapeDtypeStruct((1, tok_dev), F32)],
        fetched(kept), fetched(lax.ppermute(given, "top", SWAP)),
    )
    rows_x, rows_dy = got[:, :features], got[:, features : 2 * features]
    weight_grads = [
        jnp.einsum("rh,rd->hd", left, right, preferred_element_type=F32).astype(BF16)[None]
        for left, right in ((d_gate, rows_x), (d_up, rows_x), (scaled_act, rows_dy))
    ]
    return (grad_tokens[None], grad_prob, *weight_grads)


def solution(mesh):
    groups, experts = (mesh.shape[axis] for axis in ("dp", "expert"))
    split = Mesh(mesh.devices.reshape(groups, 2, experts // 2), ("dp", "top", "low"))
    expert = ("top", "low")
    in_specs = (
        P("dp", expert, None),
        P("dp", expert, None),
        P(None, expert),
        P(None, expert),
        P(expert, "dp", None),
        P(expert, "dp", None),
        P(expert, "dp", None),
    )
    out_specs = (
        P("dp", expert, None),
        P("dp", expert),
        P(expert, "dp", None),
        P(expert, "dp", None),
        P(expert, "dp", None),
    )
    return jax.shard_map(body, mesh=split, in_specs=in_specs, out_specs=out_specs, check_vma=False)
```

```python
import math

import jax
import jax.numpy as jnp
from jax import lax
from jax.experimental import pallas as pl
from jax.experimental.pallas import tpu as pltpu
from jax.sharding import Mesh
from jax.sharding import PartitionSpec as P

HALF_AXES = ("dp", "low")
SWAP = [(0, 1), (1, 0)]
LANES = 128
NEAR_SIZE = 2 << 20
F32, BF16 = jnp.float32, jnp.bfloat16
VMEM = pl.BlockSpec(memory_space=pltpu.VMEM)
HBM = pl.BlockSpec(memory_space=pltpu.HBM)


def dot(a, b, dims):
    return lax.dot_general(a, b, ((dims[:1], dims[1:]), ((), ())), preferred_element_type=F32)


def square(size):
    return tuple(lax.broadcasted_iota(jnp.int32, (size, size), axis) for axis in (0, 1))


def tail_kernel(route_hbm, prob_hbm, out_ref, route_v, prob_v, sems):
    tok_dev = out_ref.shape[0]
    copies = [
        pltpu.make_async_copy(route_hbm, route_v, sems.at[0]),
        pltpu.make_async_copy(prob_hbm, prob_v, sems.at[1]),
    ]
    for copy in copies:
        copy.start()
    own = lax.broadcasted_iota(jnp.int32, route_v.shape, 0) == lax.axis_index("dp")
    here, there = square(tok_dev)
    for copy in copies:
        copy.wait()
    route = jnp.sum(jnp.where(own, route_v[...].astype(F32), 0.0), axis=0, keepdims=True)
    prob = jnp.sum(jnp.where(own, prob_v[...].astype(F32), 0.0), axis=0, keepdims=True)
    route = jnp.sum(jnp.where(here == there, route, 0.0), axis=1, keepdims=True)
    prob = jnp.sum(jnp.where(here == there, prob, 0.0), axis=1, keepdims=True)
    lane = lax.broadcasted_iota(jnp.int32, (tok_dev, LANES), 1)
    out_ref[...] = jnp.where(lane == 0, prob, jnp.where(lane == 1, route, 0.0)).astype(BF16)


def load_kernel(*refs):
    ins, outs, down_v, sems = refs[:5], refs[5:11], refs[11], refs[12]
    hidden = ins[2].shape[0]
    joined = outs[2]
    places = (*outs[:2], joined.at[pl.ds(0, hidden), :], joined.at[pl.ds(hidden, hidden), :], down_v)
    copies = [pltpu.make_async_copy(a, b, sems.at[i]) for i, (a, b) in enumerate(zip(ins, places))]
    for copy in copies:
        copy.start()
    for copy in copies:
        copy.wait()
    for place, turned in zip(places[2:], outs[3:]):
        turned[...] = place[...].T


def pack_kernel(slots, *refs):
    own, other, (send_ref, pick_ref) = refs[:3], refs[3:6], refs[-2:]
    tok_dev, features = own[0].shape
    block = pick_ref.shape[0]
    groups = send_ref.shape[0] // block
    half = block // (2 * slots)
    top = lax.axis_index("top")
    here, there = square(tok_dev)
    place = lax.broadcasted_iota(jnp.int32, (block, tok_dev), 0)
    picks = []
    for tail_ref, origin in ((own[2], top), (other[2], 1 - top)):
        column = tail_ref[:, 1:2].astype(F32)
        row = jnp.sum(jnp.where(here == there, column, 0.0), axis=0, keepdims=True)
        rank = jnp.sum(jnp.where((column == row) & (here < there), 1.0, 0.0), axis=0, keepdims=True)
        low = row.astype(jnp.int32) - top * half
        target = low * (2 * slots) + origin * slots + rank.astype(jnp.int32)
        target = jnp.where((low >= 0) & (low < half), target, -1)
        picks.append((place == target).astype(F32).astype(BF16))
    pick_ref[:, :tok_dev] = picks[0]
    pick_ref[:, tok_dev:] = picks[1]
    start = 0
    for own_ref, other_ref in zip(own, other):
        end = start + own_ref.shape[1]
        sent = dot(picks[0], own_ref[...], (1, 0)) + dot(picks[1], other_ref[...], (1, 0))
        sent = sent.astype(BF16)
        for g in range(groups):
            send_ref[g * block : (g + 1) * block, start:end] = sent
        start = end


def expert_kernel(chunk, got_ref, rows_ref, gate_t, up_t, down_t, reply_ref, dg_ref, du_ref, sa_ref):
    features = rows_ref.shape[1]
    mine = lax.axis_index("dp")
    lane = lax.broadcasted_iota(jnp.int32, (chunk, LANES), 1)

    @pl.loop(0, got_ref.shape[0] // chunk)
    def _(step):
        at = pl.ds(pl.multiple_of(step * chunk, chunk), chunk)
        rows_x = got_ref[at, :features]
        rows_dy = got_ref[at, features : 2 * features]
        weight = got_ref[at, 2 * features : 2 * features + 1].astype(F32)
        gate_pre = dot(rows_x, gate_t[...], (1, 0))
        up_pre = dot(rows_x, up_t[...], (1, 0))
        back_proj = dot(rows_dy, down_t[...], (1, 0))
        sigma = jax.nn.sigmoid(gate_pre)
        swish = gate_pre * sigma
        slope = sigma * (1.0 + gate_pre * (1.0 - sigma))
        active = swish * up_pre
        d_active = weight * back_proj
        d_gate = (d_active * up_pre * slope).astype(BF16)
        d_up = (d_active * swish).astype(BF16)
        part = jnp.sum(active * back_proj, axis=1, keepdims=True)
        dg_ref[at, :] = d_gate
        du_ref[at, :] = d_up
        sa_ref[at, :] = (weight * active).astype(BF16)
        grad = dot(jnp.concatenate([d_gate, d_up], axis=1), rows_ref[...], (1, 0))
        reply_ref[at, :features] = grad.astype(BF16)
        reply_ref[at, features:] = jnp.where(lane == mine, part, 0.0).astype(BF16)


def combine_kernel(pick_ref, back_ref, own_ref, other_ref):
    total = dot(pick_ref[...], back_ref[...], (1, 0)).astype(BF16)
    own_ref[...] = total[: own_ref.shape[0]]
    other_ref[...] = total[own_ref.shape[0] :]


def finish_kernel(own_ref, other_ref, tok_ref, prob_ref):
    tok_dev, features = tok_ref.shape
    total = own_ref[...].astype(F32) + other_ref[...].astype(F32)
    tok_ref[...] = total[:, :features].astype(BF16)
    part = jnp.sum(total[:, features:], axis=1, keepdims=True)
    here, there = square(tok_dev)
    prob_ref[...] = jnp.sum(jnp.where(here == there, part, 0.0), axis=0, keepdims=True)


def near(shape, dtype=BF16):
    small = math.prod(shape) <= NEAR_SIZE
    return pltpu.VMEM(shape, dtype) if small else jax.ShapeDtypeStruct(shape, dtype)


def fetched(array):
    small = array.size <= NEAR_SIZE
    return pltpu.with_memory_space_constraint(array, pltpu.VMEM) if small else array


def far(*arrays):
    return [pltpu.with_memory_space_constraint(a, pltpu.HBM) for a in arrays]


def call(kernel, in_specs, outs, *args, scratch=(), cost=None):
    small = all(math.prod(out.shape) <= NEAR_SIZE for out in outs)
    return pl.pallas_call(
        kernel,
        in_specs=in_specs,
        scratch_shapes=scratch,
        out_specs=[VMEM] * len(outs),
        out_shape=outs,
        cost_estimate=cost,
        compiler_params=pltpu.CompilerParams(vmem_limit_bytes=(16 if small else 48) << 20),
    )(*args)


def body(tokens, cotangent, routes, gate_prob, w_gate, w_up, w_down):
    groups = lax.axis_size("dp")
    half = lax.axis_size("low")
    _, tok_dev, features = tokens.shape
    hidden = w_gate.shape[1]
    slots = tok_dev // 4
    block = half * 2 * slots
    rows = groups * block
    chunk = min(rows, 256)
    width = 2 * features + LANES

    x, dy = tokens[0], cotangent[0]
    others = [lax.ppermute(a, "top", SWAP) for a in (x, dy)]
    (tail,) = call(
        tail_kernel,
        [HBM] * 2,
        [near((tok_dev, LANES))],
        *far(routes, gate_prob),
        scratch=[
            pltpu.VMEM(routes.shape, routes.dtype),
            pltpu.VMEM(gate_prob.shape, gate_prob.dtype),
            pltpu.SemaphoreType.DMA((2,)),
        ],
    )
    others.append(lax.ppermute(tail, "top", SWAP))
    *own, joined, gate_t, up_t, down_t = call(
        load_kernel,
        [HBM] * 5,
        [near((tok_dev, features))] * 2
        + [near((2 * hidden, features))]
        + [near((features, hidden))] * 3,
        *far(x, dy, w_gate[0], w_up[0], w_down[0]),
        scratch=[pltpu.VMEM((hidden, features), BF16), pltpu.SemaphoreType.DMA((5,))],
        cost=pl.CostEstimate(flops=0, transcendentals=0, bytes_accessed=16 * hidden * features),
    )
    weights = [fetched(a) for a in (joined, gate_t, up_t, down_t)]
    send, pick = call(
        lambda *refs: pack_kernel(slots, *refs),
        [VMEM] * 10,
        [near((rows, width)), near((block, 2 * tok_dev))],
        *[fetched(a) for a in (*own, tail, *others)], *weights,
    )
    got = lax.all_to_all(send, HALF_AXES, split_axis=0, concat_axis=0, tiled=True)
    reply, d_gate, d_up, scaled_act = call(
        lambda *refs: expert_kernel(chunk, *refs),
        [VMEM] * 5,
        [near((rows, features + LANES))] + [near((rows, hidden))] * 3,
        fetched(got), *weights,
    )
    back = lax.all_to_all(reply, HALF_AXES, split_axis=0, concat_axis=0, tiled=True)
    kept, given = call(
        combine_kernel,
        [VMEM] * 2,
        [near((tok_dev, features + LANES))] * 2,
        jnp.tile(pick.T, (1, groups)), back,
    )
    grad_tokens, grad_prob = call(
        finish_kernel,
        [VMEM] * 2,
        [jax.ShapeDtypeStruct((tok_dev, features), BF16), jax.ShapeDtypeStruct((1, tok_dev), F32)],
        fetched(kept), fetched(lax.ppermute(given, "top", SWAP)),
    )
    rows_x, rows_dy = got[:, :features], got[:, features : 2 * features]
    weight_grads = [
        jnp.einsum("rh,rd->hd", left, right, preferred_element_type=F32).astype(BF16)[None]
        for left, right in ((d_gate, rows_x), (d_up, rows_x), (scaled_act, rows_dy))
    ]
    return (grad_tokens[None], grad_prob, *weight_grads)


def solution(mesh):
    groups, experts = (mesh.shape[axis] for axis in ("dp", "expert"))
    split = Mesh(mesh.devices.reshape(groups, 2, experts // 2), ("dp", "top", "low"))
    expert = ("top", "low")
    in_specs = (
        P("dp", expert, None),
        P("dp", expert, None),
        P(None, expert),
        P(None, expert),
        P(expert, "dp", None),
        P(expert, "dp", None),
        P(expert, "dp", None),
    )
    out_specs = (
        P("dp", expert, None),
        P("dp", expert),
        P(expert, "dp", None),
        P(expert, "dp", None),
        P(expert, "dp", None),
    )
    return jax.shard_map(body, mesh=split, in_specs=in_specs, out_specs=out_specs, check_vma=False)
```

```python
import math

import jax
import jax.numpy as jnp
from jax import lax
from jax.experimental import pallas as pl
from jax.experimental.pallas import tpu as pltpu
from jax.sharding import Mesh
from jax.sharding import PartitionSpec as P

HALF_AXES = ("dp", "low")
ALL_AXES = ("dp", "low", "top")
SWAP = [(0, 1), (1, 0)]
LANES = 128
NEAR_SIZE = 2 << 20
F32, BF16 = jnp.float32, jnp.bfloat16
VMEM = pl.BlockSpec(memory_space=pltpu.VMEM)
HBM = pl.BlockSpec(memory_space=pltpu.HBM)


def dot(a, b, dims):
    return lax.dot_general(a, b, ((dims[:1], dims[1:]), ((), ())), preferred_element_type=F32)


def square(size):
    return tuple(lax.broadcasted_iota(jnp.int32, (size, size), axis) for axis in (0, 1))


def join_kernel(route_hbm, prob_hbm, tok_hbm, cot_hbm, out_ref, route_v, prob_v, sems):
    tok_dev, features = tok_hbm.shape
    small = [
        pltpu.make_async_copy(route_hbm, route_v, sems.at[0]),
        pltpu.make_async_copy(prob_hbm, prob_v, sems.at[1]),
    ]
    large = [
        pltpu.make_async_copy(tok_hbm, out_ref.at[:, pl.ds(0, features)], sems.at[2]),
        pltpu.make_async_copy(cot_hbm, out_ref.at[:, pl.ds(features, features)], sems.at[3]),
    ]
    for copy in small + large:
        copy.start()
    own = lax.broadcasted_iota(jnp.int32, route_v.shape, 0) == lax.axis_index("dp")
    here, there = square(tok_dev)
    for copy in small:
        copy.wait()
    route = jnp.sum(jnp.where(own, route_v[...].astype(F32), 0.0), axis=0, keepdims=True)
    prob = jnp.sum(jnp.where(own, prob_v[...].astype(F32), 0.0), axis=0, keepdims=True)
    route = jnp.sum(jnp.where(here == there, route, 0.0), axis=1, keepdims=True)
    prob = jnp.sum(jnp.where(here == there, prob, 0.0), axis=1, keepdims=True)
    lane = lax.broadcasted_iota(jnp.int32, (tok_dev, LANES), 1)
    tail = jnp.where(lane == 0, prob, jnp.where(lane == 1, route, 0.0))
    out_ref[:, 2 * features :] = tail.astype(BF16)
    for copy in large:
        copy.wait()


def load_kernel(gate_hbm, up_hbm, down_hbm, rows_ref, gate_t, up_t, down_t, down_v, sems):
    hidden = gate_hbm.shape[0]
    places = (rows_ref.at[pl.ds(0, hidden), :], rows_ref.at[pl.ds(hidden, hidden), :], down_v)
    copies = [
        pltpu.make_async_copy(a, b, sems.at[i])
        for i, (a, b) in enumerate(zip((gate_hbm, up_hbm, down_hbm), places))
    ]
    for copy in copies:
        copy.start()
    for copy, place, turned in zip(copies, places, (gate_t, up_t, down_t)):
        copy.wait()
        turned[...] = place[...].T


def pack_kernel(slots, own_ref, other_ref, w0, w1, w2, w3, send_ref, pick_ref):
    del w0, w1, w2, w3
    tok_dev, width = own_ref.shape
    block = pick_ref.shape[0]
    groups = send_ref.shape[0] // block
    half = block // (2 * slots)
    top = lax.axis_index("top")
    here, there = square(tok_dev)
    place = lax.broadcasted_iota(jnp.int32, (block, tok_dev), 0)
    sent = jnp.zeros((block, width), F32)
    for rows_ref, origin in ((own_ref, top), (other_ref, 1 - top)):
        column = rows_ref[:, width - LANES + 1 : width - LANES + 2].astype(F32)
        row = jnp.sum(jnp.where(here == there, column, 0.0), axis=0, keepdims=True)
        rank = jnp.sum(jnp.where((column == row) & (here < there), 1.0, 0.0), axis=0, keepdims=True)
        low = row.astype(jnp.int32) - top * half
        target = low * (2 * slots) + origin * slots + rank.astype(jnp.int32)
        target = jnp.where((low >= 0) & (low < half), target, -1)
        pick = (place == target).astype(F32).astype(BF16)
        sent += dot(pick, rows_ref[...], (1, 0))
        if rows_ref is own_ref:
            upper = ((low >= half) | (low < 0)).astype(jnp.int32)
            upper = jnp.where(upper == 1, 1 - top, top)
            low = low + (top - upper) * half
            target = (low * 2 + upper) * slots + rank.astype(jnp.int32)
            pick_ref[...] = (place == target).astype(F32).astype(BF16)
    sent = sent.astype(BF16)
    for g in range(groups):
        send_ref[g * block : (g + 1) * block, :] = sent


def expert_kernel(slots, chunk, got_ref, rows_ref, gate_t, up_t, down_t, reply_ref, dg_ref, du_ref, sa_ref):
    features = rows_ref.shape[1]
    mine = lax.axis_index("dp")
    lane = lax.broadcasted_iota(jnp.int32, (chunk, LANES), 1)

    @pl.loop(0, got_ref.shape[0] // chunk)
    def _(step):
        at = pl.ds(pl.multiple_of(step * chunk, chunk), chunk)
        rows_x = got_ref[at, :features]
        rows_dy = got_ref[at, features : 2 * features]
        weight = got_ref[at, 2 * features : 2 * features + 1].astype(F32)
        gate_pre = dot(rows_x, gate_t[...], (1, 0))
        up_pre = dot(rows_x, up_t[...], (1, 0))
        back_proj = dot(rows_dy, down_t[...], (1, 0))
        sigma = jax.nn.sigmoid(gate_pre)
        swish = gate_pre * sigma
        slope = sigma * (1.0 + gate_pre * (1.0 - sigma))
        active = swish * up_pre
        d_active = weight * back_proj
        d_gate = (d_active * up_pre * slope).astype(BF16)
        d_up = (d_active * swish).astype(BF16)
        part = jnp.sum(active * back_proj, axis=1, keepdims=True)
        dg_ref[at, :] = d_gate
        du_ref[at, :] = d_up
        sa_ref[at, :] = (weight * active).astype(BF16)
        grad = dot(jnp.concatenate([d_gate, d_up], axis=1), rows_ref[...], (1, 0))
        tail = jnp.where(lane == mine, part, 0.0)
        for i in range(chunk // slots):
            to, rows = step * (chunk // slots) + i, slice(i * slots, (i + 1) * slots)
            reply_ref[to, :, :features] = grad[rows].astype(BF16)
            reply_ref[to, :, features:] = tail[rows].astype(BF16)


def unpack_kernel(pick_ref, back_ref, tok_ref, prob_ref):
    tok_dev, features = tok_ref.shape
    total = dot(pick_ref[...], back_ref[...], (1, 0))
    tok_ref[...] = total[:, :features].astype(BF16)
    part = jnp.sum(total[:, features:], axis=1, keepdims=True)
    here, there = square(tok_dev)
    prob_ref[...] = jnp.sum(jnp.where(here == there, part, 0.0), axis=0, keepdims=True)


def near(shape, dtype=BF16):
    small = math.prod(shape) <= NEAR_SIZE
    return pltpu.VMEM(shape, dtype) if small else jax.ShapeDtypeStruct(shape, dtype)


def fetched(array):
    small = array.size <= NEAR_SIZE
    return pltpu.with_memory_space_constraint(array, pltpu.VMEM) if small else array


def far(*arrays):
    return [pltpu.with_memory_space_constraint(a, pltpu.HBM) for a in arrays]


def call(kernel, in_specs, outs, *args, scratch=(), cost=None):
    small = all(math.prod(out.shape) <= NEAR_SIZE for out in outs)
    return pl.pallas_call(
        kernel,
        in_specs=in_specs,
        scratch_shapes=scratch,
        out_specs=[VMEM] * len(outs),
        out_shape=outs,
        cost_estimate=cost,
        compiler_params=pltpu.CompilerParams(vmem_limit_bytes=(16 if small else 48) << 20),
    )(*args)


def body(tokens, cotangent, routes, gate_prob, w_gate, w_up, w_down):
    groups = lax.axis_size("dp")
    half = lax.axis_size("low")
    _, tok_dev, features = tokens.shape
    hidden = w_gate.shape[1]
    slots = tok_dev // 4
    block = half * 2 * slots
    rows = groups * block
    chunk = min(rows, 256)
    width = 2 * features + LANES

    (own,) = call(
        join_kernel,
        [HBM] * 4,
        [near((tok_dev, width))],
        *far(routes, gate_prob, tokens[0], cotangent[0]),
        scratch=[
            pltpu.VMEM(routes.shape, routes.dtype),
            pltpu.VMEM(gate_prob.shape, gate_prob.dtype),
            pltpu.SemaphoreType.DMA((4,)),
        ],
    )
    other = lax.ppermute(own, "top", SWAP)
    weights = call(
        load_kernel,
        [HBM] * 3,
        [near((2 * hidden, features))] + [near((features, hidden))] * 3,
        *far(w_gate[0], w_up[0], w_down[0]),
        scratch=[pltpu.VMEM((hidden, features), BF16), pltpu.SemaphoreType.DMA((3,))],
        cost=pl.CostEstimate(flops=0, transcendentals=0, bytes_accessed=16 * hidden * features),
    )
    weights = [fetched(a) for a in weights]
    send, pick = call(
        lambda *refs: pack_kernel(slots, *refs),
        [VMEM] * 6,
        [near((rows, width)), near((block, tok_dev))],
        fetched(own), fetched(other), *weights,
    )
    got = lax.all_to_all(send, HALF_AXES, split_axis=0, concat_axis=0, tiled=True)
    reply, d_gate, d_up, scaled_act = call(
        lambda *refs: expert_kernel(slots, chunk, *refs),
        [VMEM] * 5,
        [near((rows // slots, slots, features + LANES))] + [near((rows, hidden))] * 3,
        fetched(got), *weights,
    )
    back = lax.all_to_all(reply, ALL_AXES, split_axis=0, concat_axis=0, tiled=True)
    grad_tokens, grad_prob = call(
        unpack_kernel,
        [VMEM] * 2,
        [jax.ShapeDtypeStruct((tok_dev, features), BF16), jax.ShapeDtypeStruct((1, tok_dev), F32)],
        jnp.tile(pick.T, (1, groups)), back.reshape(rows, features + LANES),
    )
    rows_x, rows_dy = got[:, :features], got[:, features : 2 * features]
    weight_grads = [
        jnp.einsum("rh,rd->hd", left, right, preferred_element_type=F32).astype(BF16)[None]
        for left, right in ((d_gate, rows_x), (d_up, rows_x), (scaled_act, rows_dy))
    ]
    return (grad_tokens[None], grad_prob, *weight_grads)


def solution(mesh):
    groups, experts = (mesh.shape[axis] for axis in ("dp", "expert"))
    split = Mesh(mesh.devices.reshape(groups, 2, experts // 2), ("dp", "top", "low"))
    expert = ("top", "low")
    in_specs = (
        P("dp", expert, None),
        P("dp", expert, None),
        P(None, expert),
        P(None, expert),
        P(expert, "dp", None),
        P(expert, "dp", None),
        P(expert, "dp", None),
    )
    out_specs = (
        P("dp", expert, None),
        P("dp", expert),
        P(expert, "dp", None),
        P(expert, "dp", None),
        P(expert, "dp", None),
    )
    return jax.shard_map(body, mesh=split, in_specs=in_specs, out_specs=out_specs, check_vma=False)
```

```python
import math

import jax
import jax.numpy as jnp
from jax import lax
from jax.experimental import pallas as pl
from jax.experimental.pallas import tpu as pltpu
from jax.sharding import Mesh
from jax.sharding import PartitionSpec as P

HALF_AXES = ("dp", "low")
ALL_AXES = ("dp", "low", "top")
SWAP = [(0, 1), (1, 0)]
LANES = 128
NEAR_SIZE = 2 << 20
F32, BF16 = jnp.float32, jnp.bfloat16
VMEM = pl.BlockSpec(memory_space=pltpu.VMEM)
HBM = pl.BlockSpec(memory_space=pltpu.HBM)


def dot(a, b, dims):
    return lax.dot_general(a, b, ((dims[:1], dims[1:]), ((), ())), preferred_element_type=F32)


def square(size):
    return tuple(lax.broadcasted_iota(jnp.int32, (size, size), axis) for axis in (0, 1))


def tail_kernel(route_hbm, prob_hbm, out_ref, route_v, prob_v, sems):
    tok_dev = out_ref.shape[0]
    copies = [
        pltpu.make_async_copy(route_hbm, route_v, sems.at[0]),
        pltpu.make_async_copy(prob_hbm, prob_v, sems.at[1]),
    ]
    for copy in copies:
        copy.start()
    own = lax.broadcasted_iota(jnp.int32, route_v.shape, 0) == lax.axis_index("dp")
    here, there = square(tok_dev)
    for copy in copies:
        copy.wait()
    route = jnp.sum(jnp.where(own, route_v[...].astype(F32), 0.0), axis=0, keepdims=True)
    prob = jnp.sum(jnp.where(own, prob_v[...].astype(F32), 0.0), axis=0, keepdims=True)
    route = jnp.sum(jnp.where(here == there, route, 0.0), axis=1, keepdims=True)
    prob = jnp.sum(jnp.where(here == there, prob, 0.0), axis=1, keepdims=True)
    lane = lax.broadcasted_iota(jnp.int32, (tok_dev, LANES), 1)
    out_ref[...] = jnp.where(lane == 0, prob, jnp.where(lane == 1, route, 0.0)).astype(BF16)


def load_kernel(*refs):
    ins, outs, down_v, sems = refs[:5], refs[5:11], refs[11], refs[12]
    hidden = ins[2].shape[0]
    joined = outs[2]
    places = (*outs[:2], joined.at[pl.ds(0, hidden), :], joined.at[pl.ds(hidden, hidden), :], down_v)
    copies = [pltpu.make_async_copy(a, b, sems.at[i]) for i, (a, b) in enumerate(zip(ins, places))]
    for copy in copies:
        copy.start()
    for copy, place, turned in zip(copies[2:], places[2:], outs[3:]):
        copy.wait()
        turned[...] = place[...].T
    for copy in copies[:2]:
        copy.wait()


def pack_kernel(slots, *refs):
    own, other, (send_ref, pick_ref) = refs[:3], refs[3:6], refs[-2:]
    tok_dev, features = own[0].shape
    block = pick_ref.shape[0]
    groups = send_ref.shape[0] // block
    half = block // (2 * slots)
    top = lax.axis_index("top")
    here, there = square(tok_dev)
    place = lax.broadcasted_iota(jnp.int32, (block, tok_dev), 0)
    picks = []
    for tail_ref, origin in ((own[2], top), (other[2], 1 - top)):
        column = tail_ref[:, 1:2].astype(F32)
        row = jnp.sum(jnp.where(here == there, column, 0.0), axis=0, keepdims=True)
        rank = jnp.sum(jnp.where((column == row) & (here < there), 1.0, 0.0), axis=0, keepdims=True)
        rank = rank.astype(jnp.int32)
        low = row.astype(jnp.int32) - top * half
        inside = (low >= 0) & (low < half)
        target = jnp.where(inside, low * (2 * slots) + origin * slots + rank, -1)
        picks.append((place == target).astype(F32).astype(BF16))
        if tail_ref is own[2]:
            upper = jnp.where(inside, top, 1 - top)
            low = low + (top - upper) * half
            target = (low * 2 + upper) * slots + rank
            pick_ref[...] = (place == target).astype(F32).astype(BF16)
    start = 0
    for own_ref, other_ref in zip(own, other):
        end = start + own_ref.shape[1]
        sent = dot(picks[0], own_ref[...], (1, 0)) + dot(picks[1], other_ref[...], (1, 0))
        sent = sent.astype(BF16)
        for g in range(groups):
            send_ref[g * block : (g + 1) * block, start:end] = sent
        start = end


def expert_kernel(slots, chunk, got_ref, rows_ref, gate_t, up_t, down_t, reply_ref, dg_ref, du_ref, sa_ref):
    features = rows_ref.shape[1]
    mine = lax.axis_index("dp")
    lane = lax.broadcasted_iota(jnp.int32, (chunk, LANES), 1)

    @pl.loop(0, got_ref.shape[0] // chunk)
    def _(step):
        at = pl.ds(pl.multiple_of(step * chunk, chunk), chunk)
        rows_x = got_ref[at, :features]
        rows_dy = got_ref[at, features : 2 * features]
        weight = got_ref[at, 2 * features : 2 * features + 1].astype(F32)
        gate_pre = dot(rows_x, gate_t[...], (1, 0))
        up_pre = dot(rows_x, up_t[...], (1, 0))
        back_proj = dot(rows_dy, down_t[...], (1, 0))
        sigma = jax.nn.sigmoid(gate_pre)
        swish = gate_pre * sigma
        slope = sigma * (1.0 + gate_pre * (1.0 - sigma))
        active = swish * up_pre
        d_active = weight * back_proj
        d_gate = (d_active * up_pre * slope).astype(BF16)
        d_up = (d_active * swish).astype(BF16)
        part = jnp.sum(active * back_proj, axis=1, keepdims=True)
        dg_ref[at, :] = d_gate
        du_ref[at, :] = d_up
        sa_ref[at, :] = (weight * active).astype(BF16)
        grad = dot(jnp.concatenate([d_gate, d_up], axis=1), rows_ref[...], (1, 0))
        tail = jnp.where(lane == mine, part, 0.0)
        for i in range(chunk // slots):
            to, rows = step * (chunk // slots) + i, slice(i * slots, (i + 1) * slots)
            reply_ref[to, :, :features] = grad[rows].astype(BF16)
            reply_ref[to, :, features:] = tail[rows].astype(BF16)


def unpack_kernel(pick_ref, back_ref, tok_ref, prob_ref):
    tok_dev, features = tok_ref.shape
    total = dot(pick_ref[...], back_ref[...], (1, 0))
    tok_ref[...] = total[:, :features].astype(BF16)
    part = jnp.sum(total[:, features:], axis=1, keepdims=True)
    here, there = square(tok_dev)
    prob_ref[...] = jnp.sum(jnp.where(here == there, part, 0.0), axis=0, keepdims=True)


def near(shape, dtype=BF16):
    small = math.prod(shape) <= NEAR_SIZE
    return pltpu.VMEM(shape, dtype) if small else jax.ShapeDtypeStruct(shape, dtype)


def fetched(array):
    small = array.size <= NEAR_SIZE
    return pltpu.with_memory_space_constraint(array, pltpu.VMEM) if small else array


def far(*arrays):
    return [pltpu.with_memory_space_constraint(a, pltpu.HBM) for a in arrays]


def call(kernel, in_specs, outs, *args, scratch=(), cost=None):
    small = all(math.prod(out.shape) <= NEAR_SIZE for out in outs)
    return pl.pallas_call(
        kernel,
        in_specs=in_specs,
        scratch_shapes=scratch,
        out_specs=[VMEM] * len(outs),
        out_shape=outs,
        cost_estimate=cost,
        compiler_params=pltpu.CompilerParams(vmem_limit_bytes=(16 if small else 48) << 20),
    )(*args)


def body(tokens, cotangent, routes, gate_prob, w_gate, w_up, w_down):
    groups = lax.axis_size("dp")
    half = lax.axis_size("low")
    _, tok_dev, features = tokens.shape
    hidden = w_gate.shape[1]
    slots = tok_dev // 4
    block = half * 2 * slots
    rows = groups * block
    chunk = min(rows, 256)
    width = 2 * features + LANES

    x, dy = tokens[0], cotangent[0]
    others = [lax.ppermute(a, "top", SWAP) for a in (x, dy)]
    (tail,) = call(
        tail_kernel,
        [HBM] * 2,
        [near((tok_dev, LANES))],
        *far(routes, gate_prob),
        scratch=[
            pltpu.VMEM(routes.shape, routes.dtype),
            pltpu.VMEM(gate_prob.shape, gate_prob.dtype),
            pltpu.SemaphoreType.DMA((2,)),
        ],
    )
    others.append(lax.ppermute(tail, "top", SWAP))
    *own, joined, gate_t, up_t, down_t = call(
        load_kernel,
        [HBM] * 5,
        [near((tok_dev, features))] * 2
        + [near((2 * hidden, features))]
        + [near((features, hidden))] * 3,
        *far(x, dy, w_gate[0], w_up[0], w_down[0]),
        scratch=[pltpu.VMEM((hidden, features), BF16), pltpu.SemaphoreType.DMA((5,))],
        cost=pl.CostEstimate(flops=0, transcendentals=0, bytes_accessed=16 * hidden * features),
    )
    weights = [fetched(a) for a in (joined, gate_t, up_t, down_t)]
    send, pick = call(
        lambda *refs: pack_kernel(slots, *refs),
        [VMEM] * 10,
        [near((rows, width)), near((block, tok_dev))],
        *[fetched(a) for a in (*own, tail, *others)], *weights,
    )
    got = lax.all_to_all(send, HALF_AXES, split_axis=0, concat_axis=0, tiled=True)
    reply, d_gate, d_up, scaled_act = call(
        lambda *refs: expert_kernel(slots, chunk, *refs),
        [VMEM] * 5,
        [near((rows // slots, slots, features + LANES))] + [near((rows, hidden))] * 3,
        fetched(got), *weights,
    )
    back = lax.all_to_all(reply, ALL_AXES, split_axis=0, concat_axis=0, tiled=True)
    grad_tokens, grad_prob = call(
        unpack_kernel,
        [VMEM] * 2,
        [jax.ShapeDtypeStruct((tok_dev, features), BF16), jax.ShapeDtypeStruct((1, tok_dev), F32)],
        jnp.tile(pick.T, (1, groups)), back.reshape(rows, features + LANES),
    )
    rows_x, rows_dy = got[:, :features], got[:, features : 2 * features]
    weight_grads = [
        jnp.einsum("rh,rd->hd", left, right, preferred_element_type=F32).astype(BF16)[None]
        for left, right in ((d_gate, rows_x), (d_up, rows_x), (scaled_act, rows_dy))
    ]
    return (grad_tokens[None], grad_prob, *weight_grads)


def solution(mesh):
    groups, experts = (mesh.shape[axis] for axis in ("dp", "expert"))
    split = Mesh(mesh.devices.reshape(groups, 2, experts // 2), ("dp", "top", "low"))
    expert = ("top", "low")
    in_specs = (
        P("dp", expert, None),
        P("dp", expert, None),
        P(None, expert),
        P(None, expert),
        P(expert, "dp", None),
        P(expert, "dp", None),
        P(expert, "dp", None),
    )
    out_specs = (
        P("dp", expert, None),
        P("dp", expert),
        P(expert, "dp", None),
        P(expert, "dp", None),
        P(expert, "dp", None),
    )
    return jax.shard_map(body, mesh=split, in_specs=in_specs, out_specs=out_specs, check_vma=False)
```

```python
import math

import jax
import jax.numpy as jnp
from jax import lax
from jax.experimental import pallas as pl
from jax.experimental.pallas import tpu as pltpu
from jax.sharding import Mesh
from jax.sharding import PartitionSpec as P

HALF_AXES = ("dp", "low")
ALL_AXES = ("dp", "low", "top")
SWAP = [(0, 1), (1, 0)]
LANES = 128
NEAR_SIZE = 2 << 20
F32, BF16 = jnp.float32, jnp.bfloat16
VMEM = pl.BlockSpec(memory_space=pltpu.VMEM)
HBM = pl.BlockSpec(memory_space=pltpu.HBM)


def dot(a, b, dims):
    return lax.dot_general(a, b, ((dims[:1], dims[1:]), ((), ())), preferred_element_type=F32)


def square(size):
    return tuple(lax.broadcasted_iota(jnp.int32, (size, size), axis) for axis in (0, 1))


def tail_kernel(route_hbm, prob_hbm, out_ref, route_v, prob_v, sems):
    tok_dev = out_ref.shape[0]
    copies = [
        pltpu.make_async_copy(route_hbm, route_v, sems.at[0]),
        pltpu.make_async_copy(prob_hbm, prob_v, sems.at[1]),
    ]
    for copy in copies:
        copy.start()
    own = lax.broadcasted_iota(jnp.int32, route_v.shape, 0) == lax.axis_index("dp")
    here, there = square(tok_dev)
    for copy in copies:
        copy.wait()
    route = jnp.sum(jnp.where(own, route_v[...].astype(F32), 0.0), axis=0, keepdims=True)
    prob = jnp.sum(jnp.where(own, prob_v[...].astype(F32), 0.0), axis=0, keepdims=True)
    route = jnp.sum(jnp.where(here == there, route, 0.0), axis=1, keepdims=True)
    prob = jnp.sum(jnp.where(here == there, prob, 0.0), axis=1, keepdims=True)
    lane = lax.broadcasted_iota(jnp.int32, (tok_dev, LANES), 1)
    out_ref[...] = jnp.where(lane == 0, prob, jnp.where(lane == 1, route, 0.0)).astype(BF16)


def load_kernel(*refs):
    ins, outs, down_v, sems = refs[:5], refs[5:10], refs[10], refs[11]
    hidden = ins[2].shape[0]
    joined = outs[2]
    places = (*outs[:2], joined.at[pl.ds(0, hidden), :], joined.at[pl.ds(hidden, hidden), :], down_v)
    copies = [pltpu.make_async_copy(a, b, sems.at[i]) for i, (a, b) in enumerate(zip(ins, places))]
    for copy in copies:
        copy.start()
    both_t, down_t = outs[3:]
    for i, (copy, place) in enumerate(zip(copies[2:], places[2:])):
        copy.wait()
        turned = down_t if i == 2 else both_t.at[:, pl.ds(i * hidden, hidden)]
        turned[...] = place[...].T
    for copy in copies[:2]:
        copy.wait()


def pack_kernel(slots, *refs):
    own, other, (send_ref, pick_ref) = refs[:3], refs[3:6], refs[-2:]
    tok_dev, features = own[0].shape
    block = pick_ref.shape[0]
    groups = send_ref.shape[0] // block
    half = block // (2 * slots)
    top = lax.axis_index("top")
    here, there = square(tok_dev)
    place = lax.broadcasted_iota(jnp.int32, (block, tok_dev), 0)
    picks = []
    for tail_ref, origin in ((own[2], top), (other[2], 1 - top)):
        column = tail_ref[:, 1:2].astype(F32)
        row = jnp.sum(jnp.where(here == there, column, 0.0), axis=0, keepdims=True)
        rank = jnp.sum(jnp.where((column == row) & (here < there), 1.0, 0.0), axis=0, keepdims=True)
        rank = rank.astype(jnp.int32)
        low = row.astype(jnp.int32) - top * half
        inside = (low >= 0) & (low < half)
        target = jnp.where(inside, low * (2 * slots) + origin * slots + rank, -1)
        picks.append((place == target).astype(F32))
        if tail_ref is own[2]:
            upper = jnp.where(inside, top, 1 - top)
            low = low + (top - upper) * half
            target = (low * 2 + upper) * slots + rank
            pick_ref[...] = (place == target).astype(F32).astype(BF16)
    picks = jnp.concatenate(picks, axis=1).astype(BF16)
    start = 0
    for own_ref, other_ref in zip(own, other):
        end = start + own_ref.shape[1]
        both = jnp.concatenate([own_ref[...], other_ref[...]], axis=0)
        sent = dot(picks, both, (1, 0)).astype(BF16)
        for g in range(groups):
            send_ref[g * block : (g + 1) * block, start:end] = sent
        start = end


def expert_kernel(slots, chunk, got_ref, rows_ref, both_t, down_t, reply_ref, dg_ref, du_ref, sa_ref):
    features = rows_ref.shape[1]
    hidden = dg_ref.shape[1]
    mine = lax.axis_index("dp")
    lane = lax.broadcasted_iota(jnp.int32, (chunk, LANES), 1)

    @pl.loop(0, got_ref.shape[0] // chunk)
    def _(step):
        at = pl.ds(pl.multiple_of(step * chunk, chunk), chunk)
        rows_x = got_ref[at, :features]
        rows_dy = got_ref[at, features : 2 * features]
        weight = got_ref[at, 2 * features : 2 * features + 1].astype(F32)
        both_pre = dot(rows_x, both_t[...], (1, 0))
        gate_pre, up_pre = both_pre[:, :hidden], both_pre[:, hidden:]
        back_proj = dot(rows_dy, down_t[...], (1, 0))
        sigma = jax.nn.sigmoid(gate_pre)
        swish = gate_pre * sigma
        slope = sigma * (1.0 + gate_pre * (1.0 - sigma))
        active = swish * up_pre
        d_active = weight * back_proj
        d_gate = (d_active * up_pre * slope).astype(BF16)
        d_up = (d_active * swish).astype(BF16)
        part = jnp.sum(active * back_proj, axis=1, keepdims=True)
        dg_ref[at, :] = d_gate
        du_ref[at, :] = d_up
        sa_ref[at, :] = (weight * active).astype(BF16)
        grad = dot(jnp.concatenate([d_gate, d_up], axis=1), rows_ref[...], (1, 0))
        tail = jnp.where(lane == mine, part, 0.0)
        for i in range(chunk // slots):
            to, rows = step * (chunk // slots) + i, slice(i * slots, (i + 1) * slots)
            reply_ref[to, :, :features] = grad[rows].astype(BF16)
            reply_ref[to, :, features:] = tail[rows].astype(BF16)


def unpack_kernel(pick_ref, back_ref, tok_ref, prob_ref):
    tok_dev, features = tok_ref.shape
    total = dot(pick_ref[...], back_ref[...], (1, 0))
    tok_ref[...] = total[:, :features].astype(BF16)
    part = jnp.sum(total[:, features:], axis=1, keepdims=True)
    here, there = square(tok_dev)
    prob_ref[...] = jnp.sum(jnp.where(here == there, part, 0.0), axis=0, keepdims=True)


def near(shape, dtype=BF16):
    small = math.prod(shape) <= NEAR_SIZE
    return pltpu.VMEM(shape, dtype) if small else jax.ShapeDtypeStruct(shape, dtype)


def fetched(array):
    small = array.size <= NEAR_SIZE
    return pltpu.with_memory_space_constraint(array, pltpu.VMEM) if small else array


def far(*arrays):
    return [pltpu.with_memory_space_constraint(a, pltpu.HBM) for a in arrays]


def call(kernel, in_specs, outs, *args, scratch=(), cost=None):
    small = all(math.prod(out.shape) <= NEAR_SIZE for out in outs)
    return pl.pallas_call(
        kernel,
        in_specs=in_specs,
        scratch_shapes=scratch,
        out_specs=[VMEM] * len(outs),
        out_shape=outs,
        cost_estimate=cost,
        compiler_params=pltpu.CompilerParams(vmem_limit_bytes=(16 if small else 48) << 20),
    )(*args)


def body(tokens, cotangent, routes, gate_prob, w_gate, w_up, w_down):
    groups = lax.axis_size("dp")
    half = lax.axis_size("low")
    _, tok_dev, features = tokens.shape
    hidden = w_gate.shape[1]
    slots = tok_dev // 4
    block = half * 2 * slots
    rows = groups * block
    chunk = min(rows, 256)
    width = 2 * features + LANES

    x, dy = tokens[0], cotangent[0]
    others = [lax.ppermute(a, "top", SWAP) for a in (x, dy)]
    (tail,) = call(
        tail_kernel,
        [HBM] * 2,
        [near((tok_dev, LANES))],
        *far(routes, gate_prob),
        scratch=[
            pltpu.VMEM(routes.shape, routes.dtype),
            pltpu.VMEM(gate_prob.shape, gate_prob.dtype),
            pltpu.SemaphoreType.DMA((2,)),
        ],
    )
    others.append(lax.ppermute(tail, "top", SWAP))
    *own, joined, both_t, down_t = call(
        load_kernel,
        [HBM] * 5,
        [near((tok_dev, features))] * 2
        + [near((2 * hidden, features)), near((features, 2 * hidden)), near((features, hidden))],
        *far(x, dy, w_gate[0], w_up[0], w_down[0]),
        scratch=[pltpu.VMEM((hidden, features), BF16), pltpu.SemaphoreType.DMA((5,))],
        cost=pl.CostEstimate(flops=0, transcendentals=0, bytes_accessed=16 * hidden * features),
    )
    weights = [fetched(a) for a in (joined, both_t, down_t)]
    send, pick = call(
        lambda *refs: pack_kernel(slots, *refs),
        [VMEM] * 9,
        [near((rows, width)), near((block, tok_dev))],
        *[fetched(a) for a in (*own, tail, *others)], *weights,
    )
    got = lax.all_to_all(send, HALF_AXES, split_axis=0, concat_axis=0, tiled=True)
    reply, d_gate, d_up, scaled_act = call(
        lambda *refs: expert_kernel(slots, chunk, *refs),
        [VMEM] * 4,
        [near((rows // slots, slots, features + LANES))] + [near((rows, hidden))] * 3,
        fetched(got), *weights,
    )
    back = lax.all_to_all(reply, ALL_AXES, split_axis=0, concat_axis=0, tiled=True)
    grad_tokens, grad_prob = call(
        unpack_kernel,
        [VMEM] * 2,
        [jax.ShapeDtypeStruct((tok_dev, features), BF16), jax.ShapeDtypeStruct((1, tok_dev), F32)],
        jnp.tile(pick.T, (1, groups)), back.reshape(rows, features + LANES),
    )
    rows_x, rows_dy = got[:, :features], got[:, features : 2 * features]
    weight_grads = [
        jnp.einsum("rh,rd->hd", left, right, preferred_element_type=F32).astype(BF16)[None]
        for left, right in ((d_gate, rows_x), (d_up, rows_x), (scaled_act, rows_dy))
    ]
    return (grad_tokens[None], grad_prob, *weight_grads)


def solution(mesh):
    groups, experts = (mesh.shape[axis] for axis in ("dp", "expert"))
    split = Mesh(mesh.devices.reshape(groups, 2, experts // 2), ("dp", "top", "low"))
    expert = ("top", "low")
    in_specs = (
        P("dp", expert, None),
        P("dp", expert, None),
        P(None, expert),
        P(None, expert),
        P(expert, "dp", None),
        P(expert, "dp", None),
        P(expert, "dp", None),
    )
    out_specs = (
        P("dp", expert, None),
        P("dp", expert),
        P(expert, "dp", None),
        P(expert, "dp", None),
        P(expert, "dp", None),
    )
    return jax.shard_map(body, mesh=split, in_specs=in_specs, out_specs=out_specs, check_vma=False)
```

```python
import math

import jax
import jax.numpy as jnp
from jax import lax
from jax.experimental import pallas as pl
from jax.experimental.pallas import tpu as pltpu
from jax.sharding import Mesh
from jax.sharding import PartitionSpec as P

HALF_AXES = ("dp", "low")
ALL_AXES = ("dp", "low", "top")
SWAP = [(0, 1), (1, 0)]
LANES = 128
NEAR_SIZE = 2 << 20
F32, BF16 = jnp.float32, jnp.bfloat16
VMEM = pl.BlockSpec(memory_space=pltpu.VMEM)
HBM = pl.BlockSpec(memory_space=pltpu.HBM)


def dot(a, b, dims):
    return lax.dot_general(a, b, ((dims[:1], dims[1:]), ((), ())), preferred_element_type=F32)


def square(size):
    return tuple(lax.broadcasted_iota(jnp.int32, (size, size), axis) for axis in (0, 1))


def load_kernel(*refs):
    ins, outs, down_v, sems = refs[:7], refs[7:14], refs[14], refs[15]
    hidden = ins[4].shape[0]
    joined = outs[4]
    places = (*outs[:4], joined.at[pl.ds(0, hidden), :], joined.at[pl.ds(hidden, hidden), :], down_v)
    copies = [pltpu.make_async_copy(a, b, sems.at[i]) for i, (a, b) in enumerate(zip(ins, places))]
    for copy in copies:
        copy.start()
    both_t, down_t = outs[5:]
    for i, (copy, place) in enumerate(zip(copies[4:], places[4:])):
        copy.wait()
        turned = down_t if i == 2 else both_t.at[:, pl.ds(i * hidden, hidden)]
        turned[...] = place[...].T
    for copy in copies[:4]:
        copy.wait()


def pack_kernel(slots, *refs):
    own, other, (send_ref, pick_ref) = refs[:4], refs[4:8], refs[-2:]
    tok_dev, features = own[0].shape
    block = pick_ref.shape[0]
    groups = send_ref.shape[0] // block
    half = block // (2 * slots)
    top = lax.axis_index("top")
    here, there = square(tok_dev)
    place = lax.broadcasted_iota(jnp.int32, (block, tok_dev), 0)
    mine = lax.broadcasted_iota(jnp.int32, own[2].shape, 0) == lax.axis_index("dp")
    picks, weights = [], 0.0
    for (_, _, route_ref, prob_ref), origin in ((own, top), (other, 1 - top)):
        row = jnp.sum(jnp.where(mine, route_ref[...].astype(F32), 0.0), axis=0, keepdims=True)
        prob = jnp.sum(jnp.where(mine, prob_ref[...].astype(F32), 0.0), axis=0, keepdims=True)
        column = jnp.sum(jnp.where(here == there, row, 0.0), axis=1, keepdims=True)
        rank = jnp.sum(jnp.where((column == row) & (here < there), 1.0, 0.0), axis=0, keepdims=True)
        rank = rank.astype(jnp.int32)
        low = row.astype(jnp.int32) - top * half
        inside = (low >= 0) & (low < half)
        target = jnp.where(inside, low * (2 * slots) + origin * slots + rank, -1)
        picks.append((place == target).astype(F32))
        weights += jnp.sum(picks[-1] * prob, axis=1, keepdims=True)
        if route_ref is own[2]:
            upper = jnp.where(inside, top, 1 - top)
            low = low + (top - upper) * half
            target = (low * 2 + upper) * slots + rank
            pick_ref[...] = (place == target).astype(F32).astype(BF16)
    picks = jnp.concatenate(picks, axis=1).astype(BF16)
    weights = jnp.broadcast_to(weights, (block, LANES)).astype(BF16)
    for g in range(groups):
        send_ref[g * block : (g + 1) * block, 2 * features :] = weights
    for i in range(2):
        both = jnp.concatenate([own[i][...], other[i][...]], axis=0)
        sent = dot(picks, both, (1, 0)).astype(BF16)
        for g in range(groups):
            send_ref[g * block : (g + 1) * block, i * features : (i + 1) * features] = sent


def expert_kernel(slots, chunk, got_ref, rows_ref, both_t, down_t, reply_ref, dg_ref, du_ref, sa_ref):
    features = rows_ref.shape[1]
    hidden = dg_ref.shape[1]
    mine = lax.axis_index("dp")
    lane = lax.broadcasted_iota(jnp.int32, (chunk, LANES), 1)

    @pl.loop(0, got_ref.shape[0] // chunk)
    def _(step):
        at = pl.ds(pl.multiple_of(step * chunk, chunk), chunk)
        rows_x = got_ref[at, :features]
        rows_dy = got_ref[at, features : 2 * features]
        weight = got_ref[at, 2 * features : 2 * features + 1].astype(F32)
        both_pre = dot(rows_x, both_t[...], (1, 0))
        gate_pre, up_pre = both_pre[:, :hidden], both_pre[:, hidden:]
        back_proj = dot(rows_dy, down_t[...], (1, 0))
        sigma = jax.nn.sigmoid(gate_pre)
        swish = gate_pre * sigma
        slope = sigma * (1.0 + gate_pre * (1.0 - sigma))
        active = swish * up_pre
        d_active = weight * back_proj
        d_gate = (d_active * up_pre * slope).astype(BF16)
        d_up = (d_active * swish).astype(BF16)
        part = jnp.sum(active * back_proj, axis=1, keepdims=True)
        dg_ref[at, :] = d_gate
        du_ref[at, :] = d_up
        sa_ref[at, :] = (weight * active).astype(BF16)
        grad = dot(jnp.concatenate([d_gate, d_up], axis=1), rows_ref[...], (1, 0))
        tail = jnp.where(lane == mine, part, 0.0)
        for i in range(chunk // slots):
            to, rows = step * (chunk // slots) + i, slice(i * slots, (i + 1) * slots)
            reply_ref[to, :, :features] = grad[rows].astype(BF16)
            reply_ref[to, :, features:] = tail[rows].astype(BF16)


def unpack_kernel(pick_ref, back_ref, tok_ref, prob_ref):
    tok_dev, features = tok_ref.shape
    total = dot(pick_ref[...], back_ref[...], (1, 0))
    tok_ref[...] = total[:, :features].astype(BF16)
    part = jnp.sum(total[:, features:], axis=1, keepdims=True)
    here, there = square(tok_dev)
    prob_ref[...] = jnp.sum(jnp.where(here == there, part, 0.0), axis=0, keepdims=True)


def near(shape, dtype=BF16):
    small = math.prod(shape) <= NEAR_SIZE
    return pltpu.VMEM(shape, dtype) if small else jax.ShapeDtypeStruct(shape, dtype)


def fetched(array):
    small = array.size <= NEAR_SIZE
    return pltpu.with_memory_space_constraint(array, pltpu.VMEM) if small else array


def far(*arrays):
    return [pltpu.with_memory_space_constraint(a, pltpu.HBM) for a in arrays]


def call(kernel, in_specs, outs, *args, scratch=(), cost=None):
    small = all(math.prod(out.shape) <= NEAR_SIZE for out in outs)
    return pl.pallas_call(
        kernel,
        in_specs=in_specs,
        scratch_shapes=scratch,
        out_specs=[VMEM] * len(outs),
        out_shape=outs,
        cost_estimate=cost,
        compiler_params=pltpu.CompilerParams(vmem_limit_bytes=(16 if small else 48) << 20),
    )(*args)


def body(tokens, cotangent, routes, gate_prob, w_gate, w_up, w_down):
    groups = lax.axis_size("dp")
    half = lax.axis_size("low")
    _, tok_dev, features = tokens.shape
    hidden = w_gate.shape[1]
    slots = tok_dev // 4
    block = half * 2 * slots
    rows = groups * block
    chunk = min(rows, 256)
    width = 2 * features + LANES

    rows_in = (tokens[0], cotangent[0], routes, gate_prob)
    others = [lax.ppermute(a, "top", SWAP) for a in rows_in]
    *own, joined, both_t, down_t = call(
        load_kernel,
        [HBM] * 7,
        [near(a.shape, a.dtype) for a in rows_in]
        + [near((2 * hidden, features)), near((features, 2 * hidden)), near((features, hidden))],
        *far(*rows_in, w_gate[0], w_up[0], w_down[0]),
        scratch=[pltpu.VMEM((hidden, features), BF16), pltpu.SemaphoreType.DMA((7,))],
        cost=pl.CostEstimate(flops=0, transcendentals=0, bytes_accessed=16 * hidden * features),
    )
    weights = [fetched(a) for a in (joined, both_t, down_t)]
    send, pick = call(
        lambda *refs: pack_kernel(slots, *refs),
        [VMEM] * 11,
        [near((rows, width)), near((block, tok_dev))],
        *[fetched(a) for a in (*own, *others)], *weights,
    )
    got = lax.all_to_all(send, HALF_AXES, split_axis=0, concat_axis=0, tiled=True)
    reply, d_gate, d_up, scaled_act = call(
        lambda *refs: expert_kernel(slots, chunk, *refs),
        [VMEM] * 4,
        [near((rows // slots, slots, features + LANES))] + [near((rows, hidden))] * 3,
        fetched(got), *weights,
    )
    back = lax.all_to_all(reply, ALL_AXES, split_axis=0, concat_axis=0, tiled=True)
    grad_tokens, grad_prob = call(
        unpack_kernel,
        [VMEM] * 2,
        [jax.ShapeDtypeStruct((tok_dev, features), BF16), jax.ShapeDtypeStruct((1, tok_dev), F32)],
        jnp.tile(pick.T, (1, groups)), back.reshape(rows, features + LANES),
    )
    rows_x, rows_dy = got[:, :features], got[:, features : 2 * features]
    weight_grads = [
        jnp.einsum("rh,rd->hd", left, right, preferred_element_type=F32).astype(BF16)[None]
        for left, right in ((d_gate, rows_x), (d_up, rows_x), (scaled_act, rows_dy))
    ]
    return (grad_tokens[None], grad_prob, *weight_grads)


def solution(mesh):
    groups, experts = (mesh.shape[axis] for axis in ("dp", "expert"))
    split = Mesh(mesh.devices.reshape(groups, 2, experts // 2), ("dp", "top", "low"))
    expert = ("top", "low")
    in_specs = (
        P("dp", expert, None),
        P("dp", expert, None),
        P(None, expert),
        P(None, expert),
        P(expert, "dp", None),
        P(expert, "dp", None),
        P(expert, "dp", None),
    )
    out_specs = (
        P("dp", expert, None),
        P("dp", expert),
        P(expert, "dp", None),
        P(expert, "dp", None),
        P(expert, "dp", None),
    )
    return jax.shard_map(body, mesh=split, in_specs=in_specs, out_specs=out_specs, check_vma=False)
```

```python
import math

import jax
import jax.numpy as jnp
from jax import lax
from jax.experimental import pallas as pl
from jax.experimental.pallas import tpu as pltpu
from jax.sharding import Mesh
from jax.sharding import PartitionSpec as P

HALF_AXES = ("dp", "low")
ALL_AXES = ("dp", "low", "top")
SWAP = [(0, 1), (1, 0)]
LANES = 128
NEAR_SIZE = 2 << 20
F32, BF16 = jnp.float32, jnp.bfloat16
VMEM = pl.BlockSpec(memory_space=pltpu.VMEM)
HBM = pl.BlockSpec(memory_space=pltpu.HBM)


def dot(a, b, dims):
    return lax.dot_general(a, b, ((dims[:1], dims[1:]), ((), ())), preferred_element_type=F32)


def square(size):
    return tuple(lax.broadcasted_iota(jnp.int32, (size, size), axis) for axis in (0, 1))


def tail_kernel(route_hbm, prob_hbm, out_ref, route_v, prob_v, sems):
    tok_dev = out_ref.shape[0]
    copies = [
        pltpu.make_async_copy(route_hbm, route_v, sems.at[0]),
        pltpu.make_async_copy(prob_hbm, prob_v, sems.at[1]),
    ]
    for copy in copies:
        copy.start()
    own = lax.broadcasted_iota(jnp.int32, route_v.shape, 0) == lax.axis_index("dp")
    here, there = square(tok_dev)
    for copy in copies:
        copy.wait()
    route = jnp.sum(jnp.where(own, route_v[...].astype(F32), 0.0), axis=0, keepdims=True)
    prob = jnp.sum(jnp.where(own, prob_v[...].astype(F32), 0.0), axis=0, keepdims=True)
    route = jnp.sum(jnp.where(here == there, route, 0.0), axis=1, keepdims=True)
    prob = jnp.sum(jnp.where(here == there, prob, 0.0), axis=1, keepdims=True)
    lane = lax.broadcasted_iota(jnp.int32, (tok_dev, LANES), 1)
    out_ref[...] = jnp.where(lane == 0, prob, jnp.where(lane == 1, route, 0.0)).astype(BF16)


def load_kernel(*refs):
    ins, outs, down_v, sems = refs[:5], refs[5:10], refs[10], refs[11]
    hidden = ins[2].shape[0]
    joined = outs[2]
    places = (*outs[:2], joined.at[pl.ds(0, hidden), :], joined.at[pl.ds(hidden, hidden), :], down_v)
    copies = [pltpu.make_async_copy(a, b, sems.at[i]) for i, (a, b) in enumerate(zip(ins, places))]
    for copy in copies:
        copy.start()
    both_t, down_t = outs[3:]
    for i, (copy, place) in enumerate(zip(copies[2:], places[2:])):
        copy.wait()
        turned = down_t if i == 2 else both_t.at[:, pl.ds(i * hidden, hidden)]
        turned[...] = place[...].T
    for copy in copies[:2]:
        copy.wait()


def pack_kernel(slots, *refs):
    own, other, (send_ref, pick_ref) = refs[:3], refs[3:6], refs[-2:]
    tok_dev, features = own[0].shape
    block = pick_ref.shape[0]
    groups = send_ref.shape[0] // block
    half = block // (2 * slots)
    top = lax.axis_index("top")
    here, there = square(tok_dev)
    place = lax.broadcasted_iota(jnp.int32, (block, tok_dev), 0)
    picks = []
    for tail_ref, origin in ((own[2], top), (other[2], 1 - top)):
        column = tail_ref[:, 1:2].astype(F32)
        row = jnp.sum(jnp.where(here == there, column, 0.0), axis=0, keepdims=True)
        rank = jnp.sum(jnp.where((column == row) & (here < there), 1.0, 0.0), axis=0, keepdims=True)
        rank = rank.astype(jnp.int32)
        low = row.astype(jnp.int32) - top * half
        inside = (low >= 0) & (low < half)
        target = jnp.where(inside, low * (2 * slots) + origin * slots + rank, -1)
        picks.append((place == target).astype(F32))
        if tail_ref is own[2]:
            upper = jnp.where(inside, top, 1 - top)
            low = low + (top - upper) * half
            target = (low * 2 + upper) * slots + rank
            pick_ref[...] = (place == target).astype(F32).astype(BF16)
    picks = jnp.concatenate(picks, axis=1).astype(BF16)
    start = 0
    for own_ref, other_ref in zip(own, other):
        end = start + own_ref.shape[1]
        both = jnp.concatenate([own_ref[...], other_ref[...]], axis=0)
        sent = dot(picks, both, (1, 0)).astype(BF16)
        for g in range(groups):
            send_ref[g * block : (g + 1) * block, start:end] = sent
        start = end


def expert_kernel(slots, chunk, got_ref, rows_ref, both_t, down_t, reply_ref, dg_ref, du_ref, sa_ref):
    features = rows_ref.shape[1]
    hidden = dg_ref.shape[1]
    mine = lax.axis_index("dp")
    lane = lax.broadcasted_iota(jnp.int32, (chunk, LANES), 1)

    @pl.loop(0, got_ref.shape[0] // chunk)
    def _(step):
        at = pl.ds(pl.multiple_of(step * chunk, chunk), chunk)
        rows_x = got_ref[at, :features]
        rows_dy = got_ref[at, features : 2 * features]
        weight = got_ref[at, 2 * features : 2 * features + 1].astype(F32)
        both_pre = dot(rows_x, both_t[...], (1, 0))
        gate_pre, up_pre = both_pre[:, :hidden], both_pre[:, hidden:]
        back_proj = dot(rows_dy, down_t[...], (1, 0))
        sigma = jax.nn.sigmoid(gate_pre)
        swish = gate_pre * sigma
        slope = sigma * (1.0 + gate_pre * (1.0 - sigma))
        active = swish * up_pre
        d_active = weight * back_proj
        d_gate = (d_active * up_pre * slope).astype(BF16)
        d_up = (d_active * swish).astype(BF16)
        part = jnp.sum(active * back_proj, axis=1, keepdims=True)
        dg_ref[at, :] = d_gate
        du_ref[at, :] = d_up
        sa_ref[at, :] = (weight * active).astype(BF16)
        grad = dot(jnp.concatenate([d_gate, d_up], axis=1), rows_ref[...], (1, 0))
        tail = jnp.where(lane == mine, part, 0.0)
        for i in range(chunk // slots):
            to, rows = step * (chunk // slots) + i, slice(i * slots, (i + 1) * slots)
            reply_ref[to, :, :features] = grad[rows].astype(BF16)
            reply_ref[to, :, features:] = tail[rows].astype(BF16)


def unpack_kernel(pick_ref, back_ref, tok_hbm, prob_hbm, tok_v, prob_v, sems):
    tok_dev, features = tok_v.shape
    half = features // 2
    part = dot(pick_ref[...], back_ref[:, features:], (1, 0))
    part = jnp.sum(part, axis=1, keepdims=True)
    here, there = square(tok_dev)
    prob_v[...] = jnp.sum(jnp.where(here == there, part, 0.0), axis=0, keepdims=True)
    copies = [pltpu.make_async_copy(prob_v, prob_hbm, sems.at[0])]
    copies[0].start()
    for i in range(2):
        at = pl.ds(i * half, half)
        tok_v[:, at] = dot(pick_ref[...], back_ref[:, at], (1, 0)).astype(BF16)
        copies.append(pltpu.make_async_copy(tok_v.at[:, at], tok_hbm.at[:, at], sems.at[i + 1]))
        copies[-1].start()
    for copy in copies:
        copy.wait()


def near(shape, dtype=BF16):
    small = math.prod(shape) <= NEAR_SIZE
    return pltpu.VMEM(shape, dtype) if small else jax.ShapeDtypeStruct(shape, dtype)


def fetched(array):
    small = array.size <= NEAR_SIZE
    return pltpu.with_memory_space_constraint(array, pltpu.VMEM) if small else array


def far(*arrays):
    return [pltpu.with_memory_space_constraint(a, pltpu.HBM) for a in arrays]


def call(kernel, in_specs, outs, *args, scratch=(), cost=None, out_spec=VMEM):
    small = all(math.prod(out.shape) <= NEAR_SIZE for out in outs)
    return pl.pallas_call(
        kernel,
        in_specs=in_specs,
        scratch_shapes=scratch,
        out_specs=[out_spec] * len(outs),
        out_shape=outs,
        cost_estimate=cost,
        compiler_params=pltpu.CompilerParams(vmem_limit_bytes=(16 if small else 48) << 20),
    )(*args)


def body(tokens, cotangent, routes, gate_prob, w_gate, w_up, w_down):
    groups = lax.axis_size("dp")
    half = lax.axis_size("low")
    _, tok_dev, features = tokens.shape
    hidden = w_gate.shape[1]
    slots = tok_dev // 4
    block = half * 2 * slots
    rows = groups * block
    chunk = min(rows, 256)
    width = 2 * features + LANES

    x, dy = tokens[0], cotangent[0]
    others = [lax.ppermute(a, "top", SWAP) for a in (x, dy)]
    (tail,) = call(
        tail_kernel,
        [HBM] * 2,
        [near((tok_dev, LANES))],
        *far(routes, gate_prob),
        scratch=[
            pltpu.VMEM(routes.shape, routes.dtype),
            pltpu.VMEM(gate_prob.shape, gate_prob.dtype),
            pltpu.SemaphoreType.DMA((2,)),
        ],
    )
    others.append(lax.ppermute(tail, "top", SWAP))
    *own, joined, both_t, down_t = call(
        load_kernel,
        [HBM] * 5,
        [near((tok_dev, features))] * 2
        + [near((2 * hidden, features)), near((features, 2 * hidden)), near((features, hidden))],
        *far(x, dy, w_gate[0], w_up[0], w_down[0]),
        scratch=[pltpu.VMEM((hidden, features), BF16), pltpu.SemaphoreType.DMA((5,))],
        cost=pl.CostEstimate(flops=0, transcendentals=0, bytes_accessed=16 * hidden * features),
    )
    weights = [fetched(a) for a in (joined, both_t, down_t)]
    send, pick = call(
        lambda *refs: pack_kernel(slots, *refs),
        [VMEM] * 9,
        [near((rows, width)), near((block, tok_dev))],
        *[fetched(a) for a in (*own, tail, *others)], *weights,
    )
    got = lax.all_to_all(send, HALF_AXES, split_axis=0, concat_axis=0, tiled=True)
    reply, d_gate, d_up, scaled_act = call(
        lambda *refs: expert_kernel(slots, chunk, *refs),
        [VMEM] * 4,
        [near((rows // slots, slots, features + LANES))] + [near((rows, hidden))] * 3,
        fetched(got), *weights,
    )
    back = lax.all_to_all(reply, ALL_AXES, split_axis=0, concat_axis=0, tiled=True)
    grad_tokens, grad_prob = call(
        unpack_kernel,
        [VMEM] * 2,
        [jax.ShapeDtypeStruct((tok_dev, features), BF16), jax.ShapeDtypeStruct((1, tok_dev), F32)],
        jnp.tile(pick.T, (1, groups)), back.reshape(rows, features + LANES),
        scratch=[
            pltpu.VMEM((tok_dev, features), BF16),
            pltpu.VMEM((1, tok_dev), F32),
            pltpu.SemaphoreType.DMA((3,)),
        ],
        out_spec=HBM,
    )
    rows_x, rows_dy = got[:, :features], got[:, features : 2 * features]
    weight_grads = [
        jnp.einsum("rh,rd->hd", left, right, preferred_element_type=F32).astype(BF16)[None]
        for left, right in ((d_gate, rows_x), (d_up, rows_x), (scaled_act, rows_dy))
    ]
    return (grad_tokens[None], grad_prob, *weight_grads)


def solution(mesh):
    groups, experts = (mesh.shape[axis] for axis in ("dp", "expert"))
    split = Mesh(mesh.devices.reshape(groups, 2, experts // 2), ("dp", "top", "low"))
    expert = ("top", "low")
    in_specs = (
        P("dp", expert, None),
        P("dp", expert, None),
        P(None, expert),
        P(None, expert),
        P(expert, "dp", None),
        P(expert, "dp", None),
        P(expert, "dp", None),
    )
    out_specs = (
        P("dp", expert, None),
        P("dp", expert),
        P(expert, "dp", None),
        P(expert, "dp", None),
        P(expert, "dp", None),
    )
    return jax.shard_map(body, mesh=split, in_specs=in_specs, out_specs=out_specs, check_vma=False)
```

```python
import math

import jax
import jax.numpy as jnp
from jax import lax
from jax.experimental import pallas as pl
from jax.experimental.pallas import tpu as pltpu
from jax.sharding import Mesh
from jax.sharding import PartitionSpec as P

HALF_AXES = ("dp", "low")
ALL_AXES = ("dp", "low", "top")
SWAP = [(0, 1), (1, 0)]
LANES = 128
NEAR_SIZE = 2 << 20
F32, BF16 = jnp.float32, jnp.bfloat16
VMEM = pl.BlockSpec(memory_space=pltpu.VMEM)
HBM = pl.BlockSpec(memory_space=pltpu.HBM)


def dot(a, b, dims):
    return lax.dot_general(a, b, ((dims[:1], dims[1:]), ((), ())), preferred_element_type=F32)


def square(size):
    return tuple(lax.broadcasted_iota(jnp.int32, (size, size), axis) for axis in (0, 1))


def tail_kernel(route_hbm, prob_hbm, out_ref, route_v, prob_v, sems):
    tok_dev = out_ref.shape[0]
    copies = [
        pltpu.make_async_copy(route_hbm, route_v, sems.at[0]),
        pltpu.make_async_copy(prob_hbm, prob_v, sems.at[1]),
    ]
    for copy in copies:
        copy.start()
    own = lax.broadcasted_iota(jnp.int32, route_v.shape, 0) == lax.axis_index("dp")
    here, there = square(tok_dev)
    for copy in copies:
        copy.wait()
    route = jnp.sum(jnp.where(own, route_v[...].astype(F32), 0.0), axis=0, keepdims=True)
    prob = jnp.sum(jnp.where(own, prob_v[...].astype(F32), 0.0), axis=0, keepdims=True)
    route = jnp.sum(jnp.where(here == there, route, 0.0), axis=1, keepdims=True)
    prob = jnp.sum(jnp.where(here == there, prob, 0.0), axis=1, keepdims=True)
    lane = lax.broadcasted_iota(jnp.int32, (tok_dev, LANES), 1)
    out_ref[...] = jnp.where(lane == 0, prob, jnp.where(lane == 1, route, 0.0)).astype(BF16)


def load_kernel(*refs):
    ins, outs, down_v, sems = refs[:5], refs[5:10], refs[10], refs[11]
    hidden = ins[2].shape[0]
    joined = outs[2]
    places = (*outs[:2], joined.at[pl.ds(0, hidden), :], joined.at[pl.ds(hidden, hidden), :], down_v)
    copies = [pltpu.make_async_copy(a, b, sems.at[i]) for i, (a, b) in enumerate(zip(ins, places))]
    for copy in copies:
        copy.start()
    both_t, down_t = outs[3:]
    for i, (copy, place) in enumerate(zip(copies[2:], places[2:])):
        copy.wait()
        turned = down_t if i == 2 else both_t.at[:, pl.ds(i * hidden, hidden)]
        turned[...] = place[...].T
    for copy in copies[:2]:
        copy.wait()


def pack_kernel(slots, *refs):
    own, other, (send_ref, pick_ref) = refs[:3], refs[3:6], refs[-2:]
    tok_dev, features = own[0].shape
    block = pick_ref.shape[0]
    groups = send_ref.shape[0] // block
    half = block // (2 * slots)
    top = lax.axis_index("top")
    here, there = square(tok_dev)
    place = lax.broadcasted_iota(jnp.int32, (block, tok_dev), 0)
    picks = []
    for tail_ref, origin in ((own[2], top), (other[2], 1 - top)):
        column = tail_ref[:, 1:2].astype(F32)
        row = jnp.sum(jnp.where(here == there, column, 0.0), axis=0, keepdims=True)
        rank = jnp.sum(jnp.where((column == row) & (here < there), 1.0, 0.0), axis=0, keepdims=True)
        rank = rank.astype(jnp.int32)
        low = row.astype(jnp.int32) - top * half
        inside = (low >= 0) & (low < half)
        target = jnp.where(inside, low * (2 * slots) + origin * slots + rank, -1)
        picks.append((place == target).astype(F32))
        if tail_ref is own[2]:
            upper = jnp.where(inside, top, 1 - top)
            low = low + (top - upper) * half
            target = (low * 2 + upper) * slots + rank
            pick_ref[...] = (place == target).astype(F32).astype(BF16)
    picks = jnp.concatenate(picks, axis=1).astype(BF16)
    start = 0
    for own_ref, other_ref in zip(own, other):
        end = start + own_ref.shape[1]
        both = jnp.concatenate([own_ref[...], other_ref[...]], axis=0)
        sent = dot(picks, both, (1, 0)).astype(BF16)
        for g in range(groups):
            send_ref[g * block : (g + 1) * block, start:end] = sent
        start = end


def expert_kernel(slots, chunk, got_ref, rows_ref, both_t, down_t, reply_ref, dg_ref, du_ref, sa_ref):
    features = rows_ref.shape[1]
    hidden = dg_ref.shape[1]
    mine = lax.axis_index("dp")
    lane = lax.broadcasted_iota(jnp.int32, (chunk, LANES), 1)

    @pl.loop(0, got_ref.shape[0] // chunk)
    def _(step):
        at = pl.ds(pl.multiple_of(step * chunk, chunk), chunk)
        rows_x = got_ref[at, :features]
        rows_dy = got_ref[at, features : 2 * features]
        weight = got_ref[at, 2 * features : 2 * features + 1].astype(F32)
        both_pre = dot(rows_x, both_t[...], (1, 0))
        gate_pre, up_pre = both_pre[:, :hidden], both_pre[:, hidden:]
        back_proj = dot(rows_dy, down_t[...], (1, 0))
        sigma = jax.nn.sigmoid(gate_pre)
        swish = gate_pre * sigma
        slope = sigma * (1.0 + gate_pre * (1.0 - sigma))
        active = swish * up_pre
        d_active = weight * back_proj
        d_gate = (d_active * up_pre * slope).astype(BF16)
        d_up = (d_active * swish).astype(BF16)
        part = jnp.sum(active * back_proj, axis=1, keepdims=True)
        dg_ref[at, :] = d_gate
        du_ref[at, :] = d_up
        sa_ref[at, :] = (weight * active).astype(BF16)
        grad = dot(jnp.concatenate([d_gate, d_up], axis=1), rows_ref[...], (1, 0))
        tail = jnp.where(lane == mine, part, 0.0)
        for i in range(chunk // slots):
            to, rows = step * (chunk // slots) + i, slice(i * slots, (i + 1) * slots)
            reply_ref[to, :, :features] = grad[rows].astype(BF16)
            reply_ref[to, :, features:] = tail[rows].astype(BF16)


def unpack_kernel(pick_ref, back_ref, tok_ref, prob_ref):
    tok_dev, features = tok_ref.shape
    back = back_ref[...].reshape(pick_ref.shape[1], back_ref.shape[2])
    total = dot(pick_ref[...], back, (1, 0))
    tok_ref[...] = total[:, :features].astype(BF16)
    part = jnp.sum(total[:, features:], axis=1, keepdims=True)
    here, there = square(tok_dev)
    prob_ref[...] = jnp.sum(jnp.where(here == there, part, 0.0), axis=0, keepdims=True)


def near(shape, dtype=BF16):
    small = math.prod(shape) <= NEAR_SIZE
    return pltpu.VMEM(shape, dtype) if small else jax.ShapeDtypeStruct(shape, dtype)


def fetched(array):
    small = array.size <= NEAR_SIZE
    return pltpu.with_memory_space_constraint(array, pltpu.VMEM) if small else array


def far(*arrays):
    return [pltpu.with_memory_space_constraint(a, pltpu.HBM) for a in arrays]


def call(kernel, in_specs, outs, *args, scratch=(), cost=None):
    small = all(math.prod(out.shape) <= NEAR_SIZE for out in outs)
    return pl.pallas_call(
        kernel,
        in_specs=in_specs,
        scratch_shapes=scratch,
        out_specs=[VMEM] * len(outs),
        out_shape=outs,
        cost_estimate=cost,
        compiler_params=pltpu.CompilerParams(vmem_limit_bytes=(16 if small else 48) << 20),
    )(*args)


def body(tokens, cotangent, routes, gate_prob, w_gate, w_up, w_down):
    groups = lax.axis_size("dp")
    half = lax.axis_size("low")
    _, tok_dev, features = tokens.shape
    hidden = w_gate.shape[1]
    slots = tok_dev // 4
    block = half * 2 * slots
    rows = groups * block
    chunk = min(rows, 256)
    width = 2 * features + LANES

    x, dy = tokens[0], cotangent[0]
    others = [lax.ppermute(a, "top", SWAP) for a in (x, dy)]
    (tail,) = call(
        tail_kernel,
        [HBM] * 2,
        [near((tok_dev, LANES))],
        *far(routes, gate_prob),
        scratch=[
            pltpu.VMEM(routes.shape, routes.dtype),
            pltpu.VMEM(gate_prob.shape, gate_prob.dtype),
            pltpu.SemaphoreType.DMA((2,)),
        ],
    )
    others.append(lax.ppermute(tail, "top", SWAP))
    *own, joined, both_t, down_t = call(
        load_kernel,
        [HBM] * 5,
        [near((tok_dev, features))] * 2
        + [near((2 * hidden, features)), near((features, 2 * hidden)), near((features, hidden))],
        *far(x, dy, w_gate[0], w_up[0], w_down[0]),
        scratch=[pltpu.VMEM((hidden, features), BF16), pltpu.SemaphoreType.DMA((5,))],
        cost=pl.CostEstimate(flops=0, transcendentals=0, bytes_accessed=16 * hidden * features),
    )
    weights = [fetched(a) for a in (joined, both_t, down_t)]
    send, pick = call(
        lambda *refs: pack_kernel(slots, *refs),
        [VMEM] * 9,
        [near((rows, width)), near((block, tok_dev))],
        *[fetched(a) for a in (*own, tail, *others)], *weights,
    )
    got = lax.all_to_all(send, HALF_AXES, split_axis=0, concat_axis=0, tiled=True)
    reply, d_gate, d_up, scaled_act = call(
        lambda *refs: expert_kernel(slots, chunk, *refs),
        [VMEM] * 4,
        [near((rows // slots, slots, features + LANES))] + [near((rows, hidden))] * 3,
        fetched(got), *weights,
    )
    back = lax.all_to_all(reply, ALL_AXES, split_axis=0, concat_axis=0, tiled=True)
    grad_tokens, grad_prob = call(
        unpack_kernel,
        [VMEM] * 2,
        [jax.ShapeDtypeStruct((tok_dev, features), BF16), jax.ShapeDtypeStruct((1, tok_dev), F32)],
        jnp.tile(pick.T, (1, groups)), back,
    )
    rows_x, rows_dy = got[:, :features], got[:, features : 2 * features]
    weight_grads = [
        jnp.einsum("rh,rd->hd", left, right, preferred_element_type=F32).astype(BF16)[None]
        for left, right in ((d_gate, rows_x), (d_up, rows_x), (scaled_act, rows_dy))
    ]
    return (grad_tokens[None], grad_prob, *weight_grads)


def solution(mesh):
    groups, experts = (mesh.shape[axis] for axis in ("dp", "expert"))
    split = Mesh(mesh.devices.reshape(groups, 2, experts // 2), ("dp", "top", "low"))
    expert = ("top", "low")
    in_specs = (
        P("dp", expert, None),
        P("dp", expert, None),
        P(None, expert),
        P(None, expert),
        P(expert, "dp", None),
        P(expert, "dp", None),
        P(expert, "dp", None),
    )
    out_specs = (
        P("dp", expert, None),
        P("dp", expert),
        P(expert, "dp", None),
        P(expert, "dp", None),
        P(expert, "dp", None),
    )
    return jax.shard_map(body, mesh=split, in_specs=in_specs, out_specs=out_specs, check_vma=False)
```
